32 devices in a mesh: groups: 2 (over y), loans: 4 (over z), paths: 4 (over x, core).
Axes of the slice: x: 2, y: 2, z: 4, core: 2. Of those that a mesh axis runs over, the one named last changes fastest.
Arguments:
- loan_features: bfloat16 [8192, 128], P(('groups', 'loans')), parts along dimension 0, may hold values from -6 to 6
- hazard_coef: bfloat16 [128, 2], replicated, may hold values from -0.5 to 0.5
- coupon: float32 [8192], P(('groups', 'loans')), parts along dimension 0, may hold values from 0.03 to 0.075
- balance: float32 [8192], P(('groups', 'loans')), parts along dimension 0, may hold values from 0.25 to 4
- loan_term: int32 [8192], P(('groups', 'loans')), parts along dimension 0, may hold values from 180 to 360
- loan_age: int32 [8192], P(('groups', 'loans')), parts along dimension 0, may hold values from 0 to 119
- loan_region: int32 [8192], P(('groups', 'loans')), parts along dimension 0, may hold values from 0 to 415
- loan_deal: int32 [8192], P(('groups', 'loans')), parts along dimension 0, may hold values from 0 to 31, as said below
- region_hpi: float32 [832, 6, 512], P(('groups', 'loans'), None, 'paths'), parts along dimension 0, may hold values from -0.6 to 0.6
- rate_paths: float32 [2, 6, 1024], P(None, None, ('groups', 'paths')), parts along dimension 2, may hold values from 0.01 to 0.08
- deal_owner: int32 [64, 1], P('groups'), parts along dimension 0, may hold values from 0 to 3; in each aligned block of 32 rows (0 to 31, 32 to 63, ...) at most 24 rows name the same one
- tranche_order: int32 [64, 64], P('groups'), parts along dimension 0, may hold values from 0 to 63, each once within a row
- tranche_share: float32 [64, 64], P('groups'), parts along dimension 0, may hold values from 0.2 to 5
- tranche_rate: float32 [64, 64], P('groups'), parts along dimension 0, may hold values from 0.02 to 0.07
Outputs:
- tranche_value: float32 [64, 64], P('groups'), parts along dimension 0
The draws below stay inside these ranges and needn't reach their ends.
There are 2 independent parts, one for each index of `groups`. The reference program is written for one: setup_inputs(seed, part) draws one part's arguments, and reference() takes and returns one part's arrays. A program takes and returns all parts, laid end to end along the dimension named above; an argument that names none is the same for every part. Nothing has to cross between parts.
Inputs may be any that keep to these rules, and one draw needn't show every extreme that they name: `loan_deal`: every deal holds at least one loan. `deal_owner`: no index of loans owns more than 24 deals, and one owns exactly 24. `tranche_order`: each row names every tranche once.
All inputs are finite; a program needn't handle non-finite values.
Results may differ from the reference program's by a relative error of at most 0.0003.
Values sent between devices are 32-bit elements; how exact they have to be, the bound alone decides.
A program may use at most 64 MiB of HBM per device.

```python
import math
import jax
import jax.numpy as jnp
import numpy as np
from jax import lax

PATH_DEV = 128
STEPS = 6
REGIONS = 416
TRANCHES = 64
FEAT = 128
DEAL_MAX = 24
LOANS = 4096
PATHS = 512
DEALS = 32
N_LOANS = 4
N_PATHS = 4


def draw_loan_deal(key, part):
    first, second = jax.random.split(jax.random.fold_in(key, 11))
    picks = jax.random.randint(first, (LOANS,), 0, DEALS).astype(jnp.int32)
    spots = jax.random.permutation(second, LOANS)[:DEALS]
    return picks.at[spots].set(jnp.arange(DEALS, dtype=jnp.int32)).astype(jnp.int32)


def set_ends(result, own_key, low, high):
    longest = result.shape.index(max(result.shape))
    spots = []
    for shift in (0, 1):
        where = [jax.random.randint(jax.random.fold_in(own_key, axis), (), 0, length) for axis, length in enumerate(result.shape)]
        where[longest] = (where[longest] + shift) % result.shape[longest]
        spots.append(tuple(where))
    return result.at[spots[0]].set(low).at[spots[1]].set(high)


def levels(rng, extent, cuts, least, top_value):
    def one(position, blocks):
        heights = jax.random.uniform(jax.random.fold_in(jax.random.fold_in(rng, 6), position), (blocks,), jnp.float32, least / len(cuts), top_value / len(cuts))
        return jnp.repeat(jnp.exp(heights), extent[position] // blocks).reshape((-1,) + (1,) * (len(extent) - position - 1))

    level = one(*cuts[0])
    for cut in cuts[1:]:
        level = level * one(*cut)
    return level


def rank_bounds(count, lean):
    weights = [(1 << 20) // math.isqrt(grade ** lean) + 1 for grade in range(1, count + 1)]
    deviation = 1 + sum(weights) // (1 << 30)
    return np.cumsum(np.array([max(1, weight // deviation) for weight in weights]))


def ranked(own_key, dims, amount, skew):
    table = rank_bounds(amount, skew)
    ticket = jax.random.randint(jax.random.fold_in(own_key, 1), dims, 0, int(table[amount - 1]))
    grade = jnp.searchsorted(jnp.asarray(table, jnp.int32), ticket, side="right")
    return jax.random.permutation(jax.random.fold_in(own_key, 2), amount)[grade].astype(jnp.int32)


def shared_out(key, own, number, rows, number_of, top, limit, slope):
    ranking = jax.random.permutation(key, number_of)
    crowded, common = load_shares(number_of, rows * top, limit, slope, True), load_shares(number_of, rows * top, limit, slope, False)
    places = jnp.arange(number_of)

    def named(tallies, rotation):
        used = int((tallies > 0).sum())
        fixed = max(1, used // 4)
        shifted = fixed + (places - fixed + rotation * (used - fixed)) % max(1, number_of - fixed)
        return jnp.zeros((number_of,), jnp.int32).at[ranking[jnp.where(places < fixed, places, shifted)]].set(jnp.asarray(tallies, jnp.int32))

    tallies = jnp.where(number % 4 == 0, named(crowded, number // 4), named(common, number - number // 4 - 1))
    mixed = jax.random.permutation(jax.random.fold_in(own, 3), number_of)
    source_of, taker = mixed[0:number_of // 2 * 2:2], mixed[1:number_of // 2 * 2:2]
    margin = jnp.minimum(tallies[source_of] - 1, limit - tallies[taker]) // 2
    margin = jnp.where((source_of == ranking[0]) | (taker == ranking[0]) | (tallies[taker] == 0), 0, jnp.maximum(margin, 0))
    shifted = jax.random.randint(jax.random.fold_in(own, 4), (number_of // 2,), 0, 1 << 20) % (margin + 1)
    tallies = tallies.at[source_of].add(-shifted).at[taker].add(shifted)
    items = jnp.searchsorted(jnp.cumsum(tallies), jnp.arange(rows * top), side="right").astype(jnp.int32)
    table = items.reshape(top, rows).T
    table = table[jax.random.permutation(jax.random.fold_in(own, 1), rows)]
    rotation = jax.random.randint(jax.random.fold_in(own, 2), (rows, 1), 0, top)
    return jnp.take_along_axis(table, (jnp.arange(top)[None, :] + rotation) % top, axis=1)


def load_shares(number_of, total, bound, lean, full):
    weights = [(1 << 20) // math.isqrt(grade ** lean) + 1 for grade in range(1, number_of + 1)]
    largest = bound if full else min(bound, max(-(-total // number_of), total * weights[0] // sum(weights)))
    least = 1 if total - largest >= number_of - 1 else 0
    holding, rest = [largest] + [least] * (number_of - 1), total - largest - least * (number_of - 1)
    while rest > 0:
        candidates = [i for i in range(1, number_of) if holding[i] < largest] or [i for i in range(1, number_of) if holding[i] < bound]
        pool, remaining = sum([weights[i] for i in candidates]), rest
        for i in candidates:
            addition = min(bound - holding[i], max(1, remaining * weights[i] // pool), rest)
            holding[i] = holding[i] + addition
            rest = rest - addition
    return np.array(holding)


def gaussian(stream_key, extent, scale, reach, pieces=(), kind=jnp.bfloat16):
    result = jax.random.normal(stream_key, extent, jnp.float32) * scale
    if len(pieces) > 0:
        result = levels(stream_key, extent, pieces, -0.22, 0.18) * result
    return jnp.clip(result, min=-reach, max=reach).astype(kind)


def setup_inputs(seed: int = 0, part: int = 0) -> dict:
    splits = jax.random.split(jax.random.key(seed), 15)
    part_splits = jax.random.split(jax.random.fold_in(splits[14], part), 15)
    loan_features = gaussian(part_splits[0], (LOANS, FEAT), 1.0, 6.0, ((0, 4),))
    hazard_coef = gaussian(splits[1], (FEAT, 2), FEAT ** -0.5, 0.5)
    coupon = jnp.clip(0.03 + 0.045 * jax.random.uniform(part_splits[2], (LOANS,), jnp.float32) ** levels(part_splits[2], (LOANS,), ((0, 4),), -0.2, 0.2), 0.03, 0.075)
    balance = jnp.clip(jnp.exp(math.log(4.0) - 2.7725887 * jax.random.uniform(part_splits[3], (LOANS,), jnp.float32) ** levels(part_splits[3], (LOANS,), ((0, 4),), -0.2, 0.2)), 0.25, 4.0)
    loan_term = set_ends(jax.random.randint(part_splits[4], (LOANS,), 180, 361), jax.random.fold_in(part_splits[4], 1), 180, 360).astype(jnp.int32)
    loan_age = set_ends(jax.random.randint(part_splits[5], (LOANS,), 0, 120), jax.random.fold_in(part_splits[5], 1), 0, 119).astype(jnp.int32)
    loan_region = set_ends(ranked(part_splits[6], (LOANS,), REGIONS, 2), jax.random.fold_in(part_splits[6], 3), 0, REGIONS - 1).astype(jnp.int32)
    loan_deal = draw_loan_deal(jax.random.fold_in(jax.random.fold_in(splits[14], part), 71), part)
    region_hpi = gaussian(part_splits[8], (REGIONS, STEPS, PATHS), 0.15, 0.6, ((0, 4), (2, 4)), jnp.float32)
    rate_paths = jnp.clip(0.01 + 0.07 * jax.random.uniform(part_splits[9], (2, STEPS, PATHS), jnp.float32) ** levels(part_splits[9], (2, STEPS, PATHS), ((2, 4),), -0.2, 0.2), 0.01, 0.08)
    deal_owner_keys = jax.random.split(jax.random.fold_in(part_splits[10], 1), DEALS // DEALS)
    deal_owner_turns = jax.random.permutation(jax.random.fold_in(part_splits[10], 3), DEALS // DEALS)
    deal_owner = jax.vmap(lambda own, number: shared_out(jax.random.fold_in(part_splits[10], 2), own, number, DEALS, N_LOANS, 1, DEAL_MAX, 2))(deal_owner_keys, deal_owner_turns).reshape((DEALS, 1))
    tranche_order = jax.vmap(lambda own: jax.random.permutation(own, TRANCHES))(jax.random.split(part_splits[11], DEALS)).reshape((DEALS, TRANCHES)).astype(jnp.int32)
    tranche_share = jnp.clip(jnp.exp(jax.random.uniform(part_splits[12], (DEALS, TRANCHES), jnp.float32, math.log(0.2), math.log(5.0))), 0.2, 5.0)
    tranche_rate = jnp.clip(jax.random.uniform(part_splits[13], (DEALS, TRANCHES), jnp.float32, 0.02, 0.07), 0.02, 0.07)
    return dict(loan_features=loan_features, hazard_coef=hazard_coef, coupon=coupon, balance=balance, loan_term=loan_term, loan_age=loan_age, loan_region=loan_region, loan_deal=loan_deal, region_hpi=region_hpi, rate_paths=rate_paths, deal_owner=deal_owner, tranche_order=tranche_order, tranche_share=tranche_share, tranche_rate=tranche_rate)


prepay_base = -4.0
incentive = 40.0
default_base = -6.0
price_sens = 12.0
oas_spread = 0.005


def loan_month(held, covar, coupon, rate_month, sched_rate, mortgage_now, hpi_now):
    smm = jax.nn.sigmoid(covar[:, 0][None, :] + prepay_base + incentive * (coupon[None, :] - mortgage_now[:, None]))
    mdr = jax.nn.sigmoid(covar[:, 1][None, :] + default_base - price_sens * hpi_now)
    interest = held * rate_month[None, :]
    sched = held * sched_rate[None, :]
    lost = mdr * held
    prepaid = smm * (held - sched - lost)
    principal = sched + prepaid + lost
    return held - principal, principal, interest


def priority_mask(tranche_order):
    count = tranche_order.shape[1]
    spots = jnp.arange(count, dtype=jnp.int32)
    hits = tranche_order[:, :, None] == spots[None, None, :]
    prio = jnp.sum(jnp.where(hits, spots[None, :, None], 0), axis=1)
    return (prio[:, :, None] < prio[:, None, :]).astype(jnp.float32)


def waterfall(princ, inter, starts, shares, rates, ahead_mask, short, valid):
    steps = princ.shape[2]
    blank = 1.0 - valid
    weights = shares / (jnp.sum(shares, axis=1, keepdims=True) + blank[:, None])
    opening = weights * starts[:, None]
    safe_open = opening + blank[:, None]
    held = jnp.broadcast_to(opening[:, None, :], (princ.shape[0], princ.shape[1], shares.shape[1]))
    decay = jnp.exp(-jnp.cumsum(short + oas_spread, axis=0) / 12.0)
    worth = jnp.zeros_like(held)
    for step in range(steps):
        ahead = jnp.einsum("xpj,xjk->xpk", held, ahead_mask, precision=lax.Precision.HIGHEST)
        paid = jnp.minimum(jnp.maximum(princ[:, :, step, None] - ahead, 0.0), held)
        coupon_due = rates[:, None, :] * held
        denom = jnp.sum(coupon_due, axis=2, keepdims=True) + blank[:, None, None]
        flow = paid + inter[:, :, step, None] * coupon_due / denom
        worth = worth + flow * decay[step][None, :, None]
        held = held - paid
    worth = worth + held * decay[steps - 1][None, :, None]
    return jnp.sum(worth / safe_open[:, None, :], axis=1)


def reference(loan_features, hazard_coef, coupon, balance, loan_term, loan_age, loan_region, loan_deal, region_hpi, rate_paths, deal_owner, tranche_order, tranche_share, tranche_rate):
    covar = jnp.dot(loan_features, hazard_coef, preferred_element_type=jnp.float32)
    rate_month = coupon / 12.0
    term_left = (loan_term - loan_age).astype(jnp.float32)
    hpi_blocks = region_hpi.reshape(REGIONS, STEPS, N_PATHS, PATH_DEV).transpose(2, 0, 1, 3)
    mort_blocks = rate_paths[1].reshape(STEPS, N_PATHS, PATH_DEV).transpose(1, 0, 2)

    def one_block(pair):
        hpi_block, mort_block = pair
        held = jnp.broadcast_to(balance[None, :], (PATH_DEV, LOANS))
        sums = []
        for step in range(STEPS):
            sched_rate = rate_month / jnp.expm1((term_left - step) * jnp.log1p(rate_month))
            hpi_now = jnp.take(hpi_block[:, step, :], loan_region, axis=0).T
            held, principal, interest = loan_month(held, covar, coupon, rate_month, sched_rate, mort_block[step], hpi_now)
            prin_deal = jax.ops.segment_sum(principal.T, loan_deal, num_segments=DEALS)
            int_deal = jax.ops.segment_sum(interest.T, loan_deal, num_segments=DEALS)
            sums.append(jnp.stack([prin_deal, int_deal], 1))
        return jnp.stack(sums, 3)

    flows = lax.map(one_block, (hpi_blocks, mort_blocks))
    flows = flows.transpose(1, 2, 0, 3, 4).reshape(DEALS, 2, PATHS, STEPS)
    starts = jax.ops.segment_sum(balance, loan_deal, num_segments=DEALS)
    ahead_mask = priority_mask(tranche_order)
    total = waterfall(flows[:, 0], flows[:, 1], starts, tranche_share, tranche_rate, ahead_mask, rate_paths[0], jnp.ones((DEALS,), jnp.float32))
    value = 100.0 * (total / PATHS - 1.0)
    order_key = deal_owner[:, 0] * DEALS + jnp.arange(DEALS, dtype=jnp.int32)
    listing = jnp.argsort(order_key)
    return value[listing]
```

```python
import functools

import jax
import jax.numpy as jnp
from jax import lax
from jax.experimental import pallas as pl
from jax.experimental.pallas import tpu as pltpu
from jax.sharding import PartitionSpec as P

prepay_base = -4.0
incentive = 40.0
default_base = -6.0
price_sens = 12.0
oas_spread = 0.005


def loan_month(held, covar, coupon, rate_month, sched_rate, mortgage_now, hpi_now):
    smm = jax.nn.sigmoid(
        covar[:, 0][None, :] + prepay_base + incentive * (coupon[None, :] - mortgage_now[:, None])
    )
    mdr = jax.nn.sigmoid(covar[:, 1][None, :] + default_base - price_sens * hpi_now)
    interest = held * rate_month[None, :]
    sched = held * sched_rate[None, :]
    lost = mdr * held
    prepaid = smm * (held - sched - lost)
    principal = sched + prepaid + lost
    return (held - principal, principal, interest)


def priority_mask(tranche_order):
    count = tranche_order.shape[1]
    spots = jnp.arange(count, dtype=jnp.int32)
    hits = tranche_order[:, :, None] == spots[None, None, :]
    prio = jnp.sum(jnp.where(hits, spots[None, :, None], 0), axis=1)
    return (prio[:, :, None] < prio[:, None, :]).astype(jnp.float32)


def waterfall(princ, inter, starts, shares, rates, ahead_mask, short, valid):
    steps = princ.shape[2]
    blank = 1.0 - valid
    weights = shares / (jnp.sum(shares, axis=1, keepdims=True) + blank[:, None])
    opening = weights * starts[:, None]
    safe_open = opening + blank[:, None]
    held = jnp.broadcast_to(opening[:, None, :], (princ.shape[0], princ.shape[1], shares.shape[1]))
    decay = []
    run = jnp.zeros_like(short[0])
    for step in range(steps):
        run = run + (short[step] + oas_spread)
        decay.append(jnp.exp(-run / 12.0))
    worth = jnp.zeros_like(held)
    for step in range(steps):
        ahead = jnp.einsum("xpj,xjk->xpk", held, ahead_mask, precision=lax.Precision.HIGHEST)
        paid = jnp.minimum(jnp.maximum(princ[:, :, step, None] - ahead, 0.0), held)
        coupon_due = rates[:, None, :] * held
        denom = jnp.sum(coupon_due, axis=2, keepdims=True) + blank[:, None, None]
        flow = paid + inter[:, :, step, None] * coupon_due / denom
        worth = worth + flow * decay[step][None, :, None]
        held = held - paid
    worth = worth + held * decay[steps - 1][None, :, None]
    return jnp.sum(worth / safe_open[:, None, :], axis=1)


def on_device(
    loan_features,
    hazard_coef,
    coupon,
    balance,
    loan_term,
    loan_age,
    loan_region,
    loan_deal,
    region_hpi,
    rate_paths,
    deal_owner,
    tranche_order,
    tranche_share,
    tranche_rate,
):
    highest = lax.Precision.HIGHEST
    loans_here = coupon.shape[0]
    paths_here = rate_paths.shape[2]
    steps = rate_paths.shape[1]
    deals = deal_owner.shape[0]
    groups = lax.axis_size("loans")
    me_loan = lax.axis_index("loans")
    covar = jnp.dot(loan_features, hazard_coef, preferred_element_type=jnp.float32)
    piece = lax.all_gather(region_hpi, "loans", axis=0, tiled=True)
    rows = piece.shape[0]
    marks = (loan_region[None, :] == lax.iota(jnp.int32, rows)[:, None]).astype(jnp.float32)
    loan_hpi = jnp.einsum("rc,rl->cl", piece.reshape(rows, -1), marks, precision=highest)
    loan_hpi = loan_hpi.reshape(steps, paths_here, loans_here)
    rate_month = coupon / 12.0
    term_left = (loan_term - loan_age).astype(jnp.float32)
    held = jnp.broadcast_to(balance[None, :], (paths_here, loans_here))
    prin_list = []
    int_list = []
    for step in range(steps):
        sched_rate = rate_month / jnp.expm1((term_left - step) * jnp.log1p(rate_month))
        held, principal, interest = loan_month(
            held, covar, coupon, rate_month, sched_rate, rate_paths[1, step], loan_hpi[step]
        )
        prin_list.append(principal)
        int_list.append(interest)
    cash = jnp.stack([jnp.stack(prin_list, 1), jnp.stack(int_list, 1)], 1)
    deal_ids = lax.iota(jnp.int32, deals)
    match = loan_deal[:, None] == deal_ids[None, :]
    onehot_deal = match.astype(jnp.float32)
    totals = lax.psum(jnp.dot(balance, onehot_deal, precision=highest), "loans")
    owners = deal_owner[:, 0]
    order_key = owners * deals + deal_ids
    position = jnp.sum((order_key[None, :] < order_key[:, None]).astype(jnp.int32), axis=1)
    place = (position[None, :] == deal_ids[:, None]).astype(jnp.float32)
    ahead_mask = priority_mask(tranche_order)
    portion = paths_here // groups
    block = cash.reshape(-1, loans_here)
    path_flows = lax.psum_scatter(
        jnp.dot(block, onehot_deal, precision=highest).reshape(
            portion * lax.axis_size("loans"), 2, steps, deals
        ),
        "loans",
        scatter_dimension=0,
        tiled=True,
    )
    flows = path_flows.transpose(3, 0, 1, 2)
    short = lax.dynamic_slice_in_dim(rate_paths[0], me_loan * portion, portion, 1)
    by_deal = waterfall(
        flows[:, :, 0, :],
        flows[:, :, 1, :],
        totals,
        tranche_share,
        tranche_rate,
        ahead_mask,
        short,
        jnp.ones((deals,), jnp.float32),
    )
    ordered = jnp.dot(place, by_deal, precision=highest)
    mine = lax.psum(ordered, "loans")
    total = lax.psum(mine, "paths")
    all_paths = paths_here * lax.axis_size("paths")
    return 100.0 * (total / all_paths - 1.0)


MESH = pl.DeviceIdType.MESH


def rows_of(x):
    return x.reshape((1,) + x.shape)


def pool_kernel(groups, lanes_out, *refs):
    n_loans, n_paths = groups
    sources, out = refs[:14], refs[14]
    feat, coef, coupon, balance, term, age, region, deal, hpi, rates, owner, order, share, trate = refs[15:29]
    (loan_tx, loan_rx, early_tx, early_rx, late_tx, late_rx, early_tab, late_tab, mort, terms, members, balances,
     early_cash, late_cash, fracs, table, cols, part, part_rx,
     in_sem, loan_ss, loan_rs, pass_ss, pass_rs, early_ss, early_rs, late_ss, late_rs, part_ss, part_rs) = refs[29:]
    f32, bf16 = jnp.float32, jnp.bfloat16
    me = lax.axis_index("loans")
    me_path = lax.axis_index("paths")
    rank = me * n_paths + me_path
    n_all = n_loans * n_paths
    n = coupon.shape[1]
    steps, rows, paths = hpi.shape
    here = paths // n_loans
    early = n_loans
    late = steps - early
    split = late_tx.shape[1]
    deals, tranches = share.shape
    copies = lanes_out // deals
    halves = n // n_paths // 128

    def other(off):
        there = lax.rem(rank + off, n_all)
        return {"loans": there // n_paths, "paths": lax.rem(there, n_paths)}

    barrier = pltpu.get_barrier_semaphore()
    loads = [pltpu.make_async_copy(a, b, in_sem.at[k]) for k, (a, b) in enumerate(zip(sources, refs[15:29]))]
    first = (8, 0, 1, 2, 3, 4, 5, 6, 7)
    for k in first:
        loads[k].start()
    for off in range(1, n_all):
        pl.semaphore_signal(barrier, inc=1, device_id=other(off), device_id_type=MESH)
    for k in range(9, 14):
        loads[k].start()
    for k in first[1:]:
        loads[k].wait()

    covar = lax.dot_general(coef[...], feat[...], (((1,), (1,)), ((), ())), preferred_element_type=f32)
    note = coupon[...]
    home = jnp.zeros((1, n), jnp.int32)
    for k in range(1, n_loans):
        home = home + jnp.where(region[...] >= k * rows, 1, 0)
    bundle = jnp.concatenate(
        [
            0.5 * (covar[0:1, :] + prepay_base + incentive * note),
            0.5 * (covar[1:2, :] + default_base),
            note / 12.0,
            balance[...],
            (term[...] - age[...]).astype(f32),
            (region[...] - home * rows).astype(f32),
            deal[...].astype(f32),
            home.astype(f32),
        ],
        axis=0,
    )
    for q in range(n_paths):
        for k in range(halves):
            at = (q * halves + k) * 128
            loan_tx[q, k] = bundle[:, at:at + 128]

    loads[8].wait()
    scale = -0.5 * price_sens

    def turn(blocks, q):
        quarter = lax.broadcasted_iota(jnp.int32, blocks[0].shape, 1) // here
        packs = None
        for t in range(n_loans):
            x = blocks[t] if t == q else pltpu.roll(blocks[t], ((t - q) % n_loans) * here, 1)
            packs = x if packs is None else jnp.where(quarter == t, x, packs)
        return packs

    blocks = [hpi[t] * scale for t in range(early)]
    for q in range(n_loans):
        early_tx[q] = turn(blocks, q)
    loan_copies, pass_copies, early_copies, late_copies = [], [], [], []
    for off in range(1, n_loans):
        there, source = lax.rem(me + off, n_loans), lax.rem(me + n_loans - off, n_loans)
        loan_copies.append(pltpu.make_async_remote_copy(
            src_ref=loan_tx.at[me_path], dst_ref=loan_rx.at[rank], send_sem=loan_ss.at[off],
            recv_sem=loan_rs.at[off], device_id={"loans": there}, device_id_type=MESH))
        slot = source * n_paths + me_path
        for hop in range(1, n_paths):
            pass_copies.append(pltpu.make_async_remote_copy(
                src_ref=loan_rx.at[slot], dst_ref=loan_rx.at[slot],
                send_sem=pass_ss.at[off, hop], recv_sem=pass_rs.at[off, hop],
                device_id={"paths": lax.rem(me_path + hop, n_paths)}, device_id_type=MESH))
        early_copies.append(pltpu.make_async_remote_copy(
            src_ref=early_tx.at[there], dst_ref=early_rx.at[me], send_sem=early_ss.at[off],
            recv_sem=early_rs.at[off], device_id={"loans": there}, device_id_type=MESH))
        late_copies.append(pltpu.make_async_remote_copy(
            src_ref=late_tx.at[there], dst_ref=late_rx.at[me], send_sem=late_ss.at[off],
            recv_sem=late_rs.at[off], device_id={"loans": there}, device_id_type=MESH))
    pl.semaphore_wait(barrier, n_all - 1)
    for copy in loan_copies:
        copy.start()
    for copy in early_copies:
        copy.start()
    pad = jnp.zeros((2 * split - rows, paths), f32)
    blocks = [hpi[early + t, 0:split, :] * scale for t in range(late)]
    blocks += [jnp.concatenate([hpi[early + t, split:rows, :] * scale, pad], axis=0) for t in range(late)]
    for q in range(n_loans):
        late_tx[q] = turn(blocks, q)
    for copy in late_copies:
        copy.start()
    early_rx[me] = early_tx[me]
    late_rx[me] = late_tx[me]
    for q in range(n_paths):
        loan_rx[me * n_paths + q] = loan_tx[q]

    for k in range(9, 14):
        loads[k].wait()
    key = (jnp.broadcast_to(owner[...], (deals, deals)) * deals
           + lax.broadcasted_iota(jnp.int32, (deals, deals), 1)).astype(f32)
    key_col = jnp.concatenate([key, jnp.zeros((128 - deals, deals), f32)], axis=0).T[:, :deals]
    below = jnp.where(key_col < key, 1.0, 0.0).astype(f32)
    spot = jnp.sum(below, axis=0, keepdims=True)
    perm = jnp.where(spot == lax.broadcasted_iota(jnp.int32, (deals, deals), 0).astype(f32), 1.0, 0.0).astype(f32)
    listing = jnp.sum(perm * lax.broadcasted_iota(jnp.int32, (deals, deals), 1).astype(f32), axis=1, keepdims=True)

    def spread(x):
        x = jnp.dot(perm, x, preferred_element_type=f32, precision=lax.Precision.HIGHEST)
        x = jnp.concatenate([x, jnp.zeros((deals, 128 - tranches), f32)], axis=1)
        return jnp.concatenate([x] * copies, axis=0).T[:tranches, :]

    table[...] = spread(order[...].astype(f32))
    share_t = spread(share[...])
    rate_t = spread(trate[...])
    names = lax.broadcasted_iota(jnp.int32, (tranches, lanes_out), 0).astype(f32)

    def walk(j, carry):
        run, upto = carry
        hit = names == table[pl.ds(j, 1), :]
        run = run + jnp.sum(jnp.where(hit, share_t, 0.0), axis=0, keepdims=True)
        return run, jnp.where(hit, run, upto)

    whole, upto = lax.fori_loop(
        0, tranches, walk, (jnp.zeros((1, lanes_out), f32), jnp.zeros((tranches, lanes_out), f32)), unroll=4)
    weight = share_t / whole
    upto = upto / whole
    per_weight = 1.0 / weight
    due_t = rate_t * weight

    stack = jnp.concatenate([rates[t] for t in range(steps)] + [jnp.zeros((128 - 2 * steps, paths), f32)], axis=0)
    cols[...] = stack.T
    mine = cols[pl.ds(pl.multiple_of(me * here, here), here), :]
    disc = []
    total = jnp.zeros((here, 1), f32)
    for t in range(steps):
        mort[t] = jnp.broadcast_to((0.5 * incentive) * mine[:, 2 * t + 1:2 * t + 2], (here, 128))
        total = total + (mine[:, 2 * t:2 * t + 1] + oas_spread)
        disc.append(jnp.exp(-total / 12.0))

    for k, copy in enumerate(loan_copies):
        copy.wait_recv()
        for again in pass_copies[k * (n_paths - 1):(k + 1) * (n_paths - 1)]:
            again.start()
    for copy in pass_copies:
        copy.wait_recv()

    ages = lax.broadcasted_iota(jnp.int32, (8, 128), 0).astype(f32)
    listed = jnp.broadcast_to(listing, (deals, 128))

    def prepare(i, sums):
        for k in range(halves):
            lv = loan_rx[i, k]
            r = lv[2:3, :]
            grown = 1.0 + r
            log = jnp.log(grown) * (r / (grown - 1.0))
            x = (lv[4:5, :] - ages) * log
            terms[i, k] = 1.0 - (2.0 * r) / (jnp.exp(x) - 1.0)
            hit = listed == lv[6:7, :]
            high = r.astype(bf16).astype(f32)
            member = jnp.concatenate(
                [jnp.where(hit, 1.0, 0.0), jnp.where(hit, high, 0.0), jnp.where(hit, r - high, 0.0),
                 jnp.zeros((lanes_out - 3 * deals, 128), f32)], axis=0).astype(bf16)
            members[i * halves + k] = member
            b = jnp.broadcast_to(lv[3:4, :], (16, 128))
            high = b.astype(bf16)
            both = jnp.concatenate([high, (b - high.astype(f32)).astype(bf16)], axis=0)
            sums = sums + lax.dot_general(both, member, (((1,), (1,)), ((), ())), preferred_element_type=f32)
        return sums

    base_sums = lax.fori_loop(0, n_all, prepare, jnp.zeros((32, lanes_out), f32))

    def months(start, count, tab, cash):
        height = count * here

        def group(i, carry):
            for k in range(halves):
                def row(ref, j):
                    return jnp.broadcast_to(ref[i, k, j:j + 1, :], (8, 128))

                lane = row(loan_rx, 5).astype(jnp.int32)
                home = row(loan_rx, 7)
                away = [home == float(c) for c in range(1, n_loans)]
                for p in range(0, here, 16):
                    pair = [[], []]
                    for b in range(2):
                        at = p + 8 * b
                        held = row(loan_rx, 3) if start == 0 else balances[i, k, at:at + 8, :]
                        for t in range(count):
                            low = t * here + at
                            h = None
                            for c in range(n_loans):
                                x = jnp.take_along_axis(
                                    tab[c, low:low + 8, :], lane, axis=1, mode="promise_in_bounds")
                                h = x if h is None else jnp.where(away[c - 1], x, h)
                            keep = ((1.0 - jnp.tanh(row(loan_rx, 0) - mort[start + t, at:at + 8, :]))
                                    * (row(terms, start + t) - jnp.tanh(row(loan_rx, 1) + h)))
                            later = held * keep
                            pair[b].append(4.0 * held - later)
                            held = later
                        if start + count < steps:
                            balances[i, k, at:at + 8, :] = held
                    for t in range(count):
                        x = jnp.concatenate([pair[0][t], pair[1][t]], axis=0)
                        high = x.astype(bf16)
                        cash[i * halves + k, t * here + p:t * here + p + 16, :] = high
                        cash[i * halves + k, height + t * here + p:height + t * here + p + 16, :] = (
                            x - high.astype(f32)).astype(bf16)
            return carry

        lax.fori_loop(0, n_all, group, 0)
        flat = jnp.concatenate([cash[g] for g in range(n_all * halves)], axis=1)
        sets = jnp.concatenate([members[g] for g in range(n_all * halves)], axis=1)
        sums = lax.dot_general(flat, sets, (((1,), (1,)), ((), ())), preferred_element_type=f32)
        sums = sums[:height] + sums[height:]
        return [sums[t * here:(t + 1) * here] * (0.25 ** (start + t + 1)) for t in range(count)]

    sub = here // copies
    group_of = lax.broadcasted_iota(jnp.int32, (sub, lanes_out), 1) // deals

    def packed(x):
        x = jnp.broadcast_to(x, (here, lanes_out))
        y = x[0:sub]
        for c in range(1, copies):
            y = jnp.where(group_of == c, x[c * sub:(c + 1) * sub], y)
        return y

    def shifted(x, column):
        pieces = [x[c * sub:(c + 1) * sub] for c in range(copies)]
        turned = [pltpu.roll(y, ((c - column) % copies) * deals, 1) if (c - column) % copies else y
                  for c, y in enumerate(pieces)]
        y = turned[0]
        for c in range(1, copies):
            y = jnp.where(group_of == c, turned[c], y)
        return y

    bases = jnp.concatenate([base_sums[0:sub] + base_sums[16:16 + sub]] * copies, axis=0)
    per_start = 1.0 / shifted(bases, 0)
    inter = shifted(bases, 1) + shifted(bases, 2)
    paid_upto = jnp.zeros((sub, lanes_out), f32)
    fall = [packed(disc[t]) for t in range(steps)]

    def waterfall_months(start, pools, inter, paid_upto, worth):
        gone, gains = [], []
        for x in pools:
            paid_upto = paid_upto + jnp.maximum(shifted(x, 0), 0.0)
            gone.append(paid_upto * per_start)
            gains.append(inter * per_start)
            inter = inter - (shifted(x, 1) + shifted(x, 2))
        end = start + len(pools) == steps
        for j in range(sub):
            frac = jnp.ones((tranches, lanes_out), f32) if start == 0 else fracs[j]
            for t in range(len(pools)):
                d = fall[start + t][j:j + 1, :]
                later = jnp.clip((upto - gone[t][j:j + 1, :]) * per_weight, 0.0, 1.0)
                denom = jnp.sum(due_t * frac, axis=0, keepdims=True)
                worth = worth + (frac - later) * d + (rate_t * frac) * (gains[t][j:j + 1, :] * d / denom)
                frac = later
            if end:
                worth = worth + frac * d
            else:
                fracs[j] = frac
        return inter, paid_upto, worth

    for copy in early_copies:
        copy.wait_recv()
    tail = jnp.zeros((128 - rows, paths), f32)
    for c in range(n_loans):
        early_tab[c] = jnp.concatenate([early_rx[c], tail], axis=0).T
    pools = months(0, early, early_tab, early_cash)
    inter, paid_upto, worth = waterfall_months(
        0, pools, inter, paid_upto, jnp.zeros((tranches, lanes_out), f32))

    for copy in late_copies:
        copy.wait_recv()
    lower = late * here
    for c in range(n_loans):
        x = jnp.concatenate([late_rx[c], jnp.zeros((128 - split, paths), f32)], axis=0).T
        upper = pltpu.roll(x[lower:], split, 1)
        late_tab[c] = jnp.where(lax.broadcasted_iota(jnp.int32, (lower, 128), 1) < split, x[:lower], upper)
    pools = months(early, late, late_tab, late_cash)
    inter, paid_upto, worth = waterfall_months(early, pools, inter, paid_upto, worth)

    wt = jnp.concatenate([worth, jnp.zeros((128 - tranches, lanes_out), f32)], axis=0).T
    acc = wt[0:deals]
    low = lax.broadcasted_iota(jnp.int32, (deals // 2, 128), 1) < 64
    for c in range(1, copies):
        acc = acc + wt[c * deals:(c + 1) * deals]
    acc = jnp.where(low, acc[:deals // 2], pltpu.roll(acc[deals // 2:], 64, 1))
    part[...] = acc
    part_copies = []
    for off in range(1, n_all):
        part_copies.append(pltpu.make_async_remote_copy(
            src_ref=part, dst_ref=part_rx.at[rank], send_sem=part_ss.at[off], recv_sem=part_rs.at[off],
            device_id=other(off), device_id_type=MESH))
    for copy in part_copies:
        copy.start()
    part_rx[rank] = acc
    for copy in part_copies:
        copy.wait_recv()
    acc = part_rx[0]
    for k in range(1, n_all):
        acc = acc + part_rx[k]
    acc = 100.0 * (acc / (paths * n_paths) - 1.0)
    out[:deals // 2, :] = acc[:, :tranches]
    out[deals // 2:, :] = pltpu.roll(acc, 64, 1)[:, :tranches]
    for copy in loan_copies + pass_copies + early_copies + late_copies + part_copies:
        copy.wait_send()


def fused(loan_features, hazard_coef, coupon, balance, loan_term, loan_age, loan_region, loan_deal,
          region_hpi, rate_paths, deal_owner, tranche_order, tranche_share, tranche_rate):
    n_loans, n_paths = lax.axis_size("loans"), lax.axis_size("paths")
    n = coupon.shape[0]
    rows, steps, paths = region_hpi.shape
    deals, tranches = tranche_share.shape
    here = paths // n_loans
    lanes_out = 128
    split = -(-rows // 16) * 8
    early, late = n_loans, steps - n_loans
    halves = n // n_paths // 128
    n_all = n_loans * n_paths
    f32, bf16 = jnp.float32, jnp.bfloat16
    dma = pltpu.SemaphoreType.DMA
    operands = (loan_features, hazard_coef.T, rows_of(coupon), rows_of(balance), rows_of(loan_term), rows_of(loan_age),
                rows_of(loan_region), rows_of(loan_deal), region_hpi.transpose(1, 0, 2),
                rate_paths.transpose(1, 0, 2), deal_owner.reshape(1, deals), tranche_order, tranche_share, tranche_rate)
    return pl.pallas_call(
        functools.partial(pool_kernel, (n_loans, n_paths), lanes_out),
        out_shape=pltpu.VMEM((deals, tranches), f32),
        in_specs=[pl.BlockSpec(memory_space=pl.ANY)] * len(operands),
        out_specs=pl.BlockSpec(memory_space=pltpu.VMEM),
        scratch_shapes=[pltpu.VMEM(x.shape, x.dtype) for x in operands] + [
            pltpu.VMEM((n_paths, halves, 8, 128), f32),
            pltpu.VMEM((n_all, halves, 8, 128), f32),
            pltpu.VMEM((n_loans, rows, paths), f32),
            pltpu.VMEM((n_loans, rows, paths), f32),
            pltpu.VMEM((n_loans, split, paths), f32),
            pltpu.VMEM((n_loans, split, paths), f32),
            pltpu.VMEM((n_loans, early * here, 128), f32),
            pltpu.VMEM((n_loans, late * here, 128), f32),
            pltpu.VMEM((steps, here, 128), f32),
            pltpu.VMEM((n_all, halves, 8, 128), f32),
            pltpu.VMEM((n_all * halves, lanes_out, 128), bf16),
            pltpu.VMEM((n_all, halves, here, 128), f32),
            pltpu.VMEM((n_all * halves, 2 * early * here, 128), bf16),
            pltpu.VMEM((n_all * halves, 2 * late * here, 128), bf16),
            pltpu.VMEM((here * deals // lanes_out, tranches, lanes_out), f32),
            pltpu.VMEM((tranches, lanes_out), f32),
            pltpu.VMEM((paths, 128), f32),
            pltpu.VMEM((deals // 2, 128), f32),
            pltpu.VMEM((n_all, deals // 2, 128), f32),
            dma((len(operands),)),
            dma((n_loans,)), dma((n_loans,)), dma((n_loans, n_paths)), dma((n_loans, n_paths)),
            dma((n_loans,)), dma((n_loans,)), dma((n_loans,)), dma((n_loans,)),
            dma((n_all,)), dma((n_all,)),
        ],
        compiler_params=pltpu.CompilerParams(collective_id=0, has_side_effects=True),
    )(*operands)


def fits(args):
    n = args[2].shape[0]
    paths = args[8].shape[2]
    deals, tranches = args[12].shape
    n_loans = lax.axis_size("loans")
    rows, steps = args[8].shape[:2]
    return (
        paths == 128 and n_loans == 4 and 2 * (steps - n_loans) == n_loans and rows % 8 == 0 and 64 < rows <= 128
        and deals in (16, 32) and tranches == 64
        and (paths // n_loans) % (8 * (128 // deals)) == 0
        and n % (128 * lax.axis_size("paths")) == 0 and n <= 2048
    )


def device_program(*args):
    return fused(*args) if fits(args) else on_device(*args)


def solution(mesh):
    in_specs = (
        P(("groups", "loans"), None),
        P(),
        P(("groups", "loans")),
        P(("groups", "loans")),
        P(("groups", "loans")),
        P(("groups", "loans")),
        P(("groups", "loans")),
        P(("groups", "loans")),
        P(("groups", "loans"), None, "paths"),
        P(None, None, ("groups", "paths")),
        P("groups", None),
        P("groups", None),
        P("groups", None),
        P("groups", None),
    )
    out_specs = P("groups", None)
    return jax.shard_map(
        device_program, mesh=mesh, in_specs=in_specs, out_specs=out_specs, check_vma=False
    )
```

```python
import functools

import jax
import jax.numpy as jnp
from jax import lax
from jax.experimental import pallas as pl
from jax.experimental.pallas import tpu as pltpu
from jax.sharding import PartitionSpec as P

prepay_base = -4.0
incentive = 40.0
default_base = -6.0
price_sens = 12.0
oas_spread = 0.005
fixed_point = 54000.0
EARLY_SPAN = 2
LATE_SPAN = 2


def loan_month(held, covar, coupon, rate_month, sched_rate, mortgage_now, hpi_now):
    smm = jax.nn.sigmoid(
        covar[:, 0][None, :] + prepay_base + incentive * (coupon[None, :] - mortgage_now[:, None])
    )
    mdr = jax.nn.sigmoid(covar[:, 1][None, :] + default_base - price_sens * hpi_now)
    interest = held * rate_month[None, :]
    sched = held * sched_rate[None, :]
    lost = mdr * held
    prepaid = smm * (held - sched - lost)
    principal = sched + prepaid + lost
    return (held - principal, principal, interest)


def priority_mask(tranche_order):
    count = tranche_order.shape[1]
    spots = jnp.arange(count, dtype=jnp.int32)
    hits = tranche_order[:, :, None] == spots[None, None, :]
    prio = jnp.sum(jnp.where(hits, spots[None, :, None], 0), axis=1)
    return (prio[:, :, None] < prio[:, None, :]).astype(jnp.float32)


def waterfall(princ, inter, starts, shares, rates, ahead_mask, short, valid):
    steps = princ.shape[2]
    blank = 1.0 - valid
    weights = shares / (jnp.sum(shares, axis=1, keepdims=True) + blank[:, None])
    opening = weights * starts[:, None]
    safe_open = opening + blank[:, None]
    held = jnp.broadcast_to(opening[:, None, :], (princ.shape[0], princ.shape[1], shares.shape[1]))
    decay = []
    run = jnp.zeros_like(short[0])
    for step in range(steps):
        run = run + (short[step] + oas_spread)
        decay.append(jnp.exp(-run / 12.0))
    worth = jnp.zeros_like(held)
    for step in range(steps):
        ahead = jnp.einsum("xpj,xjk->xpk", held, ahead_mask, precision=lax.Precision.HIGHEST)
        paid = jnp.minimum(jnp.maximum(princ[:, :, step, None] - ahead, 0.0), held)
        coupon_due = rates[:, None, :] * held
        denom = jnp.sum(coupon_due, axis=2, keepdims=True) + blank[:, None, None]
        flow = paid + inter[:, :, step, None] * coupon_due / denom
        worth = worth + flow * decay[step][None, :, None]
        held = held - paid
    worth = worth + held * decay[steps - 1][None, :, None]
    return jnp.sum(worth / safe_open[:, None, :], axis=1)


def on_device(
    loan_features,
    hazard_coef,
    coupon,
    balance,
    loan_term,
    loan_age,
    loan_region,
    loan_deal,
    region_hpi,
    rate_paths,
    deal_owner,
    tranche_order,
    tranche_share,
    tranche_rate,
):
    highest = lax.Precision.HIGHEST
    loans_here = coupon.shape[0]
    paths_here = rate_paths.shape[2]
    steps = rate_paths.shape[1]
    deals = deal_owner.shape[0]
    groups = lax.axis_size("loans")
    me_loan = lax.axis_index("loans")
    covar = jnp.dot(loan_features, hazard_coef, preferred_element_type=jnp.float32)
    piece = lax.all_gather(region_hpi, "loans", axis=0, tiled=True)
    rows = piece.shape[0]
    marks = (loan_region[None, :] == lax.iota(jnp.int32, rows)[:, None]).astype(jnp.float32)
    loan_hpi = jnp.einsum("rc,rl->cl", piece.reshape(rows, -1), marks, precision=highest)
    loan_hpi = loan_hpi.reshape(steps, paths_here, loans_here)
    rate_month = coupon / 12.0
    term_left = (loan_term - loan_age).astype(jnp.float32)
    held = jnp.broadcast_to(balance[None, :], (paths_here, loans_here))
    prin_list = []
    int_list = []
    for step in range(steps):
        sched_rate = rate_month / jnp.expm1((term_left - step) * jnp.log1p(rate_month))
        held, principal, interest = loan_month(
            held, covar, coupon, rate_month, sched_rate, rate_paths[1, step], loan_hpi[step]
        )
        prin_list.append(principal)
        int_list.append(interest)
    cash = jnp.stack([jnp.stack(prin_list, 1), jnp.stack(int_list, 1)], 1)
    deal_ids = lax.iota(jnp.int32, deals)
    match = loan_deal[:, None] == deal_ids[None, :]
    onehot_deal = match.astype(jnp.float32)
    totals = lax.psum(jnp.dot(balance, onehot_deal, precision=highest), "loans")
    owners = deal_owner[:, 0]
    order_key = owners * deals + deal_ids
    position = jnp.sum((order_key[None, :] < order_key[:, None]).astype(jnp.int32), axis=1)
    place = (position[None, :] == deal_ids[:, None]).astype(jnp.float32)
    ahead_mask = priority_mask(tranche_order)
    portion = paths_here // groups
    block = cash.reshape(-1, loans_here)
    path_flows = lax.psum_scatter(
        jnp.dot(block, onehot_deal, precision=highest).reshape(
            portion * lax.axis_size("loans"), 2, steps, deals
        ),
        "loans",
        scatter_dimension=0,
        tiled=True,
    )
    flows = path_flows.transpose(3, 0, 1, 2)
    short = lax.dynamic_slice_in_dim(rate_paths[0], me_loan * portion, portion, 1)
    by_deal = waterfall(
        flows[:, :, 0, :],
        flows[:, :, 1, :],
        totals,
        tranche_share,
        tranche_rate,
        ahead_mask,
        short,
        jnp.ones((deals,), jnp.float32),
    )
    ordered = jnp.dot(place, by_deal, precision=highest)
    mine = lax.psum(ordered, "loans")
    total = lax.psum(mine, "paths")
    all_paths = paths_here * lax.axis_size("paths")
    return 100.0 * (total / all_paths - 1.0)


MESH = pl.DeviceIdType.MESH


def rows_of(x):
    return x.reshape((1,) + x.shape)


def pool_kernel(groups, lanes_out, *refs):
    n_loans, n_paths = groups
    sources, out = refs[:14], refs[14]
    feat, coef, coupon, balance, term, age, region, deal, hpi, rates, owner, order, share, trate = refs[15:29]
    (loan_tx, loan_rx, early_tx, early_rx, late_tx, late_rx, early_tab, late_tab, mort, terms, late_stay, members, balances,
     early_cash, late_cash, early_sums, late_sums, fracs, falls, worth, table, cols, part, part_rx,
     in_sem, loan_ss, loan_rs, pass_ss, pass_rs, early_ss, early_rs, late_ss, late_rs, part_ss, part_rs) = refs[29:]
    f32, bf16 = jnp.float32, jnp.bfloat16
    me = lax.axis_index("loans")
    me_path = lax.axis_index("paths")
    rank = me * n_paths + me_path
    n_all = n_loans * n_paths
    n = coupon.shape[1]
    steps, rows, paths = hpi.shape
    here = paths // n_loans
    early = n_loans
    late = steps - early
    split = late_tx.shape[1]
    deals, tranches = share.shape
    copies = lanes_out // deals
    halves = n // n_paths // 128

    def other(off):
        there = lax.rem(rank + off, n_all)
        return {"loans": there // n_paths, "paths": lax.rem(there, n_paths)}

    barrier = pltpu.get_barrier_semaphore()
    loads = [pltpu.make_async_copy(a, b, in_sem.at[k]) for k, (a, b) in enumerate(zip(sources, refs[15:29]))]
    for off in range(1, n_loans):
        pl.semaphore_signal(barrier, inc=1, device_id={"loans": lax.rem(me + off, n_loans)}, device_id_type=MESH)
    for off in range(1, n_paths):
        pl.semaphore_signal(barrier, inc=1, device_id={"paths": lax.rem(me_path + off, n_paths)}, device_id_type=MESH)
    first = (0, 8, 1, 2, 3, 4, 5, 6, 7)
    for k in first + tuple(range(9, 14)):
        loads[k].start()
    for k in first:
        if k != 8:
            loads[k].wait()

    covar = lax.dot_general(coef[...], feat[...], (((1,), (1,)), ((), ())), preferred_element_type=f32)
    note = coupon[...]
    home = jnp.zeros((1, n), jnp.int32)
    for k in range(1, n_loans):
        home = home + jnp.where(region[...] >= k * rows, 1, 0)
    bundle = jnp.concatenate(
        [
            0.5 * (covar[0:1, :] + prepay_base + incentive * note),
            0.5 * (covar[1:2, :] + default_base),
            note / 12.0,
            balance[...],
            (term[...] - age[...]).astype(f32),
            (region[...] - home * rows).astype(f32),
            deal[...].astype(f32),
            home.astype(f32),
        ],
        axis=0,
    )
    for q in range(n_paths):
        for k in range(halves):
            at = (q * halves + k) * 128
            loan_tx[q, k] = bundle[:, at:at + 128]

    loads[8].wait()

    def turn(blocks):
        quarter = lax.broadcasted_iota(jnp.int32, blocks[0].shape, 1) // here
        half, odd = quarter < 2, quarter % 2 == 1
        swapped = [pltpu.roll(x, 2 * here, 1) for x in blocks]
        blocks = ([jnp.where(half, blocks[t], swapped[t + 2]) for t in range(2)]
                  + [jnp.where(half, swapped[t], blocks[t + 2]) for t in range(2)])
        turned = []
        for t in (0, 2):
            turned.append(jnp.where(odd, pltpu.roll(blocks[t + 1], here, 1), blocks[t]))
            turned.append(jnp.where(odd, blocks[t + 1], pltpu.roll(blocks[t], paths - here, 1)))
        return turned

    for q, block in enumerate(turn([hpi[t] for t in range(early)])):
        early_tx[q] = block
    loan_copies, pass_copies, early_copies, late_copies = [], [], [], []
    for off in range(1, n_loans):
        there, source = lax.rem(me + off, n_loans), lax.rem(me + n_loans - off, n_loans)
        loan_copies.append(pltpu.make_async_remote_copy(
            src_ref=loan_tx.at[me_path], dst_ref=loan_rx.at[rank], send_sem=loan_ss.at[off],
            recv_sem=loan_rs.at[off], device_id={"loans": there}, device_id_type=MESH))
        slot = source * n_paths + me_path
        for hop in range(1, n_paths):
            pass_copies.append(pltpu.make_async_remote_copy(
                src_ref=loan_rx.at[slot], dst_ref=loan_rx.at[slot],
                send_sem=pass_ss.at[off, hop], recv_sem=pass_rs.at[off, hop],
                device_id={"paths": lax.rem(me_path + hop, n_paths)}, device_id_type=MESH))
        early_copies.append(pltpu.make_async_remote_copy(
            src_ref=early_tx.at[there], dst_ref=early_rx.at[me], send_sem=early_ss.at[off],
            recv_sem=early_rs.at[off], device_id={"loans": there}, device_id_type=MESH))
        late_copies.append(pltpu.make_async_remote_copy(
            src_ref=late_tx.at[there], dst_ref=late_rx.at[me], send_sem=late_ss.at[off],
            recv_sem=late_rs.at[off], device_id={"loans": there}, device_id_type=MESH))
    pl.semaphore_wait(barrier, n_loans + n_paths - 2)
    for copy in loan_copies:
        copy.start()
    for copy in early_copies:
        copy.start()
    pad = jnp.zeros((2 * split - rows, paths), f32)
    blocks = [hpi[early + t, 0:split, :] for t in range(late)]
    blocks += [jnp.concatenate([hpi[early + t, split:rows, :], pad], axis=0) for t in range(late)]
    for q, block in enumerate(turn(blocks)):
        late_tx[q] = block
    for copy in late_copies:
        copy.start()
    early_rx[me] = early_tx[me]
    late_rx[me] = late_tx[me]
    for q in range(n_paths):
        loan_rx[me * n_paths + q] = loan_tx[q]

    for k in range(9, 14):
        loads[k].wait()
    key = (jnp.broadcast_to(owner[...], (deals, deals)) * deals
           + lax.broadcasted_iota(jnp.int32, (deals, deals), 1)).astype(f32)
    key_col = jnp.concatenate([key, jnp.zeros((128 - deals, deals), f32)], axis=0).T[:, :deals]
    below = jnp.where(key_col < key, 1.0, 0.0).astype(f32)
    spot = jnp.sum(below, axis=0, keepdims=True)
    perm = jnp.where(spot == lax.broadcasted_iota(jnp.int32, (deals, deals), 0).astype(f32), 1.0, 0.0).astype(f32)
    listing = jnp.sum(perm * lax.broadcasted_iota(jnp.int32, (deals, deals), 1).astype(f32), axis=1, keepdims=True)

    def spread(x):
        x = jnp.dot(perm, x, preferred_element_type=f32, precision=lax.Precision.HIGHEST)
        x = jnp.concatenate([x, jnp.zeros((deals, 128 - tranches), f32)], axis=1)
        return jnp.concatenate([x] * copies, axis=0).T[:tranches, :]

    table[...] = spread(order[...].astype(f32))
    share_t = spread(share[...])
    rate_t = spread(trate[...])
    names = lax.broadcasted_iota(jnp.int32, (tranches, lanes_out), 0).astype(f32)

    def walk(j, carry):
        run, upto = carry
        hit = names == table[pl.ds(j, 1), :]
        run = run + jnp.sum(jnp.where(hit, share_t, 0.0), axis=0, keepdims=True)
        return run, jnp.where(hit, run, upto)

    whole, upto = lax.fori_loop(
        0, tranches, walk, (jnp.zeros((1, lanes_out), f32), jnp.zeros((tranches, lanes_out), f32)), unroll=4)
    weight = share_t / whole
    upto = upto / whole
    per_weight = 1.0 / weight
    falls[0], falls[1], falls[2], falls[3] = upto, per_weight, rate_t * weight, rate_t

    stack = jnp.concatenate([rates[t] for t in range(steps)] + [jnp.zeros((128 - 2 * steps, paths), f32)], axis=0)
    cols[...] = stack.T
    mine = cols[pl.ds(pl.multiple_of(me * here, here), here), :]
    disc = []
    total = jnp.zeros((here, 1), f32)
    for t in range(steps):
        mort[t] = jnp.broadcast_to((0.5 * incentive) * mine[:, 2 * t + 1:2 * t + 2], (here, 128))
        total = total + (mine[:, 2 * t:2 * t + 1] + oas_spread)
        disc.append(jnp.exp(-total / 12.0))

    for k, copy in enumerate(loan_copies):
        copy.wait_recv()
        for again in pass_copies[k * (n_paths - 1):(k + 1) * (n_paths - 1)]:
            again.start()
    for copy in pass_copies:
        copy.wait_recv()

    ages = lax.broadcasted_iota(jnp.int32, (8, 128), 0).astype(f32)
    listed = jnp.broadcast_to(listing, (deals, 128))

    def prepare(i, sums):
        for k in range(halves):
            lv = loan_rx[i, k]
            r = lv[2:3, :]
            grown = 1.0 + r
            log = jnp.log(grown) * (r / (grown - 1.0))
            x = (lv[4:5, :] - ages) * log
            terms[i, k] = 1.0 - (2.0 * r) / (jnp.exp(x) - 1.0)
            hit = listed == lv[6:7, :]
            high = r.astype(bf16).astype(f32)
            member = jnp.concatenate(
                [jnp.where(hit, 1.0, 0.0), jnp.where(hit, high, 0.0), jnp.where(hit, r - high, 0.0),
                 jnp.zeros((lanes_out - 3 * deals, 128), f32)], axis=0).astype(bf16)
            members[i * halves + k] = member
            for t in range(late):
                late_stay[i, k, t * here:(t + 1) * here, :] = 1.0 - jnp.tanh(lv[0:1, :] - mort[early + t])
            b = jnp.broadcast_to(lv[3:4, :], (16, 128))
            high = b.astype(bf16)
            both = jnp.concatenate([high, (b - high.astype(f32)).astype(bf16)], axis=0)
            sums = sums + lax.dot_general(both, member, (((1,), (1,)), ((), ())), preferred_element_type=f32)
        return sums

    base_sums = lax.fori_loop(0, n_all, prepare, jnp.zeros((32, lanes_out), f32))

    step_scale = -0.5 * price_sens / (fixed_point * 65536.0)

    def pairs(x):
        x = jnp.floor(x * fixed_point + 0.5).astype(jnp.int32)
        return [(x[t * here:(t + 1) * here] << 16) | (x[(t + 1) * here:(t + 2) * here] & 65535)
                for t in range(0, x.shape[0] // here, 2)]

    def months(start, count, tab, cash, acc, span):
        height = count * here
        cash[0] = jnp.zeros(cash.shape[1:], bf16)
        acc[...] = jnp.zeros_like(acc)

        def slots(ref, base):
            return jnp.concatenate([ref[base + g] for g in range(span * halves)], axis=1)

        def gather_sums(i):
            flat = jnp.concatenate([cash[i, g] for g in range(span * halves)], axis=1)
            sets = slots(members, jnp.maximum(i - 1, 0) * span * halves)
            return lax.dot_general(flat, sets, (((1,), (1,)), ((), ())), preferred_element_type=f32)

        def step(i, carry):
            acc[...] += gather_sums(i)
            for g in range(span * halves):
                s, k = i * span + g // halves, g % halves

                def row(ref, j):
                    return jnp.broadcast_to(ref[s, k, j:j + 1, :], (8, 128))

                lane = row(loan_rx, 5).astype(jnp.int32)
                home = row(loan_rx, 7)
                away = [home == float(c) for c in range(1, n_loans)]
                for p in range(0, here, 16):
                    duo = [[], []]
                    for b in range(2):
                        at = p + 8 * b
                        held = row(loan_rx, 3) if start == 0 else balances[s, k, at:at + 8, :]
                        for two in range(0, count, 2):
                            low = (two // 2) * here + at
                            v = None
                            for c in range(n_loans):
                                x = jnp.take_along_axis(
                                    tab[c, low:low + 8, :], lane, axis=1, mode="promise_in_bounds")
                                v = x if v is None else jnp.where(away[c - 1], x, v)
                            for t, x in ((two, v & -65536), (two + 1, v << 16)):
                                if start == 0:
                                    stay = 1.0 - jnp.tanh(row(loan_rx, 0) - mort[t, at:at + 8, :])
                                else:
                                    stay = late_stay[s, k, t * here + at:t * here + at + 8, :]
                                alive = row(terms, start + t) - jnp.tanh(row(loan_rx, 1) + x.astype(f32) * step_scale)
                                held = held * (stay * alive)
                                duo[b].append(held)
                        if start + count < steps:
                            balances[s, k, at:at + 8, :] = held
                    for t in range(count):
                        x = jnp.concatenate([duo[0][t], duo[1][t]], axis=0)
                        high = x.astype(bf16)
                        cash[i + 1, g, t * here + p:t * here + p + 16, :] = high
                        cash[i + 1, g, height + t * here + p:height + t * here + p + 16, :] = (
                            x - high.astype(f32)).astype(bf16)
            return carry

        turns = n_all // span
        lax.fori_loop(0, turns, step, 0)
        sums = acc[...] + gather_sums(turns)
        sums = sums[:height] + sums[height:]
        return [sums[t * here:(t + 1) * here] * (0.25 ** (start + t + 1)) for t in range(count)]

    sub = here // copies
    group_of = lax.broadcasted_iota(jnp.int32, (sub, lanes_out), 1) // deals

    def packed(x):
        x = jnp.broadcast_to(x, (here, lanes_out))
        y = x[0:sub]
        for c in range(1, copies):
            y = jnp.where(group_of == c, x[c * sub:(c + 1) * sub], y)
        return y

    def shifted(x, column):
        pieces = [x[c * sub:(c + 1) * sub] for c in range(copies)]
        turned = [pltpu.roll(y, ((c - column) % copies) * deals, 1) if (c - column) % copies else y
                  for c, y in enumerate(pieces)]
        y = turned[0]
        for c in range(1, copies):
            y = jnp.where(group_of == c, turned[c], y)
        return y

    bases = jnp.concatenate([base_sums[0:sub] + base_sums[16:16 + sub]] * copies, axis=0)
    per_start = 1.0 / shifted(bases, 0)
    fall = [packed(disc[t]) for t in range(steps)]

    def flows(state, sums):
        held, inter, paid_upto = state
        gone, gains = [], []
        for x in sums:
            after = shifted(x, 0)
            paid_upto = paid_upto + jnp.maximum(held - after, 0.0)
            gone.append(paid_upto * per_start)
            gains.append(inter * per_start)
            held, inter = after, shifted(x, 1) + shifted(x, 2)
        return (held, inter, paid_upto), gone, gains

    def tall(x, j):
        return jnp.broadcast_to(x[j:j + 1, :], (8, lanes_out))

    def incomes(gain, d, dues):
        return [jnp.broadcast_to((gain[j:j + 1, :] * d[j:j + 1, :]) / jnp.sum(dues[j], axis=0, keepdims=True), (8, lanes_out))
                for j in range(sub)]

    strips = [slice(k, k + 8) for k in range(0, tranches, 8)]

    def blank():
        return [jnp.zeros((8, lanes_out), f32) for _ in range(sub)]

    def settle(first, gone, d, extra):
        gone, d, dues = [tall(gone, j) for j in range(sub)], [tall(d, j) for j in range(sub)], blank()
        for k in strips:
            w = jnp.zeros((8, lanes_out), f32) if first else worth[k, :]
            for j in range(sub):
                frac = 1.0 if first else fracs[j, k, :]
                later = jnp.clip((falls[0, k, :] - gone[j]) * falls[1, k, :], 0.0, 1.0)
                w = w + (frac - later) * d[j] + (falls[3, k, :] * frac) * extra[j]
                dues[j] = dues[j] + falls[2, k, :] * later
                fracs[j, k, :] = later
            worth[k, :] = w
        return dues

    for copy in early_copies:
        copy.wait_recv()
    tail = jnp.zeros((128 - rows, paths), f32)
    for c in range(n_loans):
        for k, x in enumerate(pairs(jnp.concatenate([early_rx[c], tail], axis=0).T)):
            early_tab[c, k * here:(k + 1) * here, :] = x
    sums = months(0, early, early_tab, early_cash, early_sums, EARLY_SPAN)
    state = (shifted(bases, 0), shifted(bases, 1) + shifted(bases, 2), jnp.zeros((sub, lanes_out), f32))
    state, gone, gains = flows(state, sums)
    dues = [sum(falls[2, k, :] for k in strips)] * sub
    for t in range(early):
        dues = settle(t == 0, gone[t], fall[t], incomes(gains[t], fall[t], dues))
    extra = incomes(state[1] * per_start, fall[early], dues)
    d = [tall(fall[early], j) for j in range(sub)]
    for k in strips:
        w = worth[k, :]
        for j in range(sub):
            w = w + fracs[j, k, :] * (d[j] + falls[3, k, :] * extra[j])
        worth[k, :] = w

    for copy in late_copies:
        copy.wait_recv()
    lower = late * here
    for c in range(n_loans):
        x = jnp.concatenate([late_rx[c], jnp.zeros((128 - split, paths), f32)], axis=0).T
        upper = pltpu.roll(x[lower:], split, 1)
        late_tab[c] = pairs(jnp.where(lax.broadcasted_iota(jnp.int32, (lower, 128), 1) < split, x[:lower], upper))[0]
    sums = months(early, late, late_tab, late_cash, late_sums, LATE_SPAN)
    state, gone, gains = flows(state, sums)
    dues = blank()
    up = [tall(gone[0], j) for j in range(sub)]
    for k in strips:
        w = worth[k, :]
        for j in range(sub):
            later = jnp.clip((falls[0, k, :] - up[j]) * falls[1, k, :], 0.0, 1.0)
            w = w - later * d[j]
            dues[j] = dues[j] + falls[2, k, :] * later
            fracs[j, k, :] = later
        worth[k, :] = w
    extra = incomes(gains[1], fall[steps - 1], dues)
    up, d = [tall(gone[1], j) for j in range(sub)], [tall(fall[steps - 1], j) for j in range(sub)]
    total = []
    for k in strips:
        w = worth[k, :]
        for j in range(sub):
            frac = fracs[j, k, :]
            later = jnp.clip((falls[0, k, :] - up[j]) * falls[1, k, :], 0.0, 1.0)
            w = w + (frac - later) * d[j] + (falls[3, k, :] * frac) * extra[j] + later * d[j]
        total.append(w)

    wt = jnp.concatenate(total + [jnp.zeros((128 - tranches, lanes_out), f32)], axis=0).T
    acc = wt[0:deals]
    low = lax.broadcasted_iota(jnp.int32, (deals // 2, 128), 1) < 64
    for c in range(1, copies):
        acc = acc + wt[c * deals:(c + 1) * deals]
    acc = jnp.where(low, acc[:deals // 2], pltpu.roll(acc[deals // 2:], 64, 1))
    part[...] = acc
    part_copies = []
    for off in range(1, n_all):
        part_copies.append(pltpu.make_async_remote_copy(
            src_ref=part, dst_ref=part_rx.at[rank], send_sem=part_ss.at[off], recv_sem=part_rs.at[off],
            device_id=other(off), device_id_type=MESH))
    for copy in part_copies:
        copy.start()
    part_rx[rank] = acc
    for copy in part_copies:
        copy.wait_recv()
    acc = part_rx[0]
    for k in range(1, n_all):
        acc = acc + part_rx[k]
    acc = 100.0 * (acc / (paths * n_paths) - 1.0)
    out[:deals // 2, :] = acc[:, :tranches]
    out[deals // 2:, :] = pltpu.roll(acc, 64, 1)[:, :tranches]
    for copy in loan_copies + pass_copies + early_copies + late_copies + part_copies:
        copy.wait_send()


def fused(loan_features, hazard_coef, coupon, balance, loan_term, loan_age, loan_region, loan_deal,
          region_hpi, rate_paths, deal_owner, tranche_order, tranche_share, tranche_rate):
    n_loans, n_paths = lax.axis_size("loans"), lax.axis_size("paths")
    n = coupon.shape[0]
    rows, steps, paths = region_hpi.shape
    deals, tranches = tranche_share.shape
    here = paths // n_loans
    lanes_out = 128
    split = -(-rows // 16) * 8
    early, late = n_loans, steps - n_loans
    halves = n // n_paths // 128
    n_all = n_loans * n_paths
    f32, bf16 = jnp.float32, jnp.bfloat16
    dma = pltpu.SemaphoreType.DMA
    operands = (loan_features, hazard_coef.T, rows_of(coupon), rows_of(balance), rows_of(loan_term), rows_of(loan_age),
                rows_of(loan_region), rows_of(loan_deal), region_hpi.transpose(1, 0, 2),
                rate_paths.transpose(1, 0, 2), deal_owner.reshape(1, deals), tranche_order, tranche_share, tranche_rate)
    return pl.pallas_call(
        functools.partial(pool_kernel, (n_loans, n_paths), lanes_out),
        out_shape=pltpu.VMEM((deals, tranches), f32),
        in_specs=[pl.BlockSpec(memory_space=pl.ANY)] * len(operands),
        out_specs=pl.BlockSpec(memory_space=pltpu.VMEM),
        scratch_shapes=[pltpu.VMEM(x.shape, x.dtype) for x in operands] + [
            pltpu.VMEM((n_paths, halves, 8, 128), f32),
            pltpu.VMEM((n_all, halves, 8, 128), f32),
            pltpu.VMEM((n_loans, rows, paths), f32),
            pltpu.VMEM((n_loans, rows, paths), f32),
            pltpu.VMEM((n_loans, split, paths), f32),
            pltpu.VMEM((n_loans, split, paths), f32),
            pltpu.VMEM((n_loans, early // 2 * here, 128), jnp.int32),
            pltpu.VMEM((n_loans, late // 2 * here, 128), jnp.int32),
            pltpu.VMEM((steps, here, 128), f32),
            pltpu.VMEM((n_all, halves, 8, 128), f32),
            pltpu.VMEM((n_all, halves, late * here, 128), f32),
            pltpu.VMEM((n_all * halves, lanes_out, 128), bf16),
            pltpu.VMEM((n_all, halves, here, 128), f32),
            pltpu.VMEM((n_all // EARLY_SPAN + 1, EARLY_SPAN * halves, 2 * early * here, 128), bf16),
            pltpu.VMEM((n_all // LATE_SPAN + 1, LATE_SPAN * halves, 2 * late * here, 128), bf16),
            pltpu.VMEM((2 * early * here, lanes_out), f32),
            pltpu.VMEM((2 * late * here, lanes_out), f32),
            pltpu.VMEM((here * deals // lanes_out, tranches, lanes_out), f32),
            pltpu.VMEM((4, tranches, lanes_out), f32),
            pltpu.VMEM((tranches, lanes_out), f32),
            pltpu.VMEM((tranches, lanes_out), f32),
            pltpu.VMEM((paths, 128), f32),
            pltpu.VMEM((deals // 2, 128), f32),
            pltpu.VMEM((n_all, deals // 2, 128), f32),
            dma((len(operands),)),
            dma((n_loans,)), dma((n_loans,)), dma((n_loans, n_paths)), dma((n_loans, n_paths)),
            dma((n_loans,)), dma((n_loans,)), dma((n_loans,)), dma((n_loans,)),
            dma((n_all,)), dma((n_all,)),
        ],
        compiler_params=pltpu.CompilerParams(collective_id=0, has_side_effects=True),
    )(*operands)


def fits(args):
    n = args[2].shape[0]
    paths = args[8].shape[2]
    deals, tranches = args[12].shape
    n_loans = lax.axis_size("loans")
    rows, steps = args[8].shape[:2]
    return (
        paths == 128 and n_loans == 4 and 2 * (steps - n_loans) == n_loans and rows % 8 == 0 and 64 < rows <= 128
        and deals in (16, 32) and tranches == 64
        and (paths // n_loans) % (8 * (128 // deals)) == 0
        and n % (128 * lax.axis_size("paths")) == 0 and n <= 2048
    )


def device_program(*args):
    return fused(*args) if fits(args) else on_device(*args)


def solution(mesh):
    in_specs = (
        P(("groups", "loans"), None),
        P(),
        P(("groups", "loans")),
        P(("groups", "loans")),
        P(("groups", "loans")),
        P(("groups", "loans")),
        P(("groups", "loans")),
        P(("groups", "loans")),
        P(("groups", "loans"), None, "paths"),
        P(None, None, ("groups", "paths")),
        P("groups", None),
        P("groups", None),
        P("groups", None),
        P("groups", None),
    )
    out_specs = P("groups", None)
    return jax.shard_map(
        device_program, mesh=mesh, in_specs=in_specs, out_specs=out_specs, check_vma=False
    )
```

```python
import functools

import jax
import jax.numpy as jnp
from jax import lax
from jax.experimental import pallas as pl
from jax.experimental.pallas import tpu as pltpu
from jax.sharding import PartitionSpec as P

prepay_base = -4.0
incentive = 40.0
default_base = -6.0
price_sens = 12.0
oas_spread = 0.005
fixed_point = 54000.0
PREPARE = 4
EARLY_SPAN = 4
LATE_SPAN = 4


def loan_month(held, covar, coupon, rate_month, sched_rate, mortgage_now, hpi_now):
    smm = jax.nn.sigmoid(
        covar[:, 0][None, :] + prepay_base + incentive * (coupon[None, :] - mortgage_now[:, None])
    )
    mdr = jax.nn.sigmoid(covar[:, 1][None, :] + default_base - price_sens * hpi_now)
    interest = held * rate_month[None, :]
    sched = held * sched_rate[None, :]
    lost = mdr * held
    prepaid = smm * (held - sched - lost)
    principal = sched + prepaid + lost
    return (held - principal, principal, interest)


def priority_mask(tranche_order):
    count = tranche_order.shape[1]
    spots = jnp.arange(count, dtype=jnp.int32)
    hits = tranche_order[:, :, None] == spots[None, None, :]
    prio = jnp.sum(jnp.where(hits, spots[None, :, None], 0), axis=1)
    return (prio[:, :, None] < prio[:, None, :]).astype(jnp.float32)


def waterfall(princ, inter, starts, shares, rates, ahead_mask, short, valid):
    steps = princ.shape[2]
    blank = 1.0 - valid
    weights = shares / (jnp.sum(shares, axis=1, keepdims=True) + blank[:, None])
    opening = weights * starts[:, None]
    safe_open = opening + blank[:, None]
    held = jnp.broadcast_to(opening[:, None, :], (princ.shape[0], princ.shape[1], shares.shape[1]))
    decay = []
    run = jnp.zeros_like(short[0])
    for step in range(steps):
        run = run + (short[step] + oas_spread)
        decay.append(jnp.exp(-run / 12.0))
    worth = jnp.zeros_like(held)
    for step in range(steps):
        ahead = jnp.einsum("xpj,xjk->xpk", held, ahead_mask, precision=lax.Precision.HIGHEST)
        paid = jnp.minimum(jnp.maximum(princ[:, :, step, None] - ahead, 0.0), held)
        coupon_due = rates[:, None, :] * held
        denom = jnp.sum(coupon_due, axis=2, keepdims=True) + blank[:, None, None]
        flow = paid + inter[:, :, step, None] * coupon_due / denom
        worth = worth + flow * decay[step][None, :, None]
        held = held - paid
    worth = worth + held * decay[steps - 1][None, :, None]
    return jnp.sum(worth / safe_open[:, None, :], axis=1)


def on_device(
    loan_features,
    hazard_coef,
    coupon,
    balance,
    loan_term,
    loan_age,
    loan_region,
    loan_deal,
    region_hpi,
    rate_paths,
    deal_owner,
    tranche_order,
    tranche_share,
    tranche_rate,
):
    highest = lax.Precision.HIGHEST
    loans_here = coupon.shape[0]
    paths_here = rate_paths.shape[2]
    steps = rate_paths.shape[1]
    deals = deal_owner.shape[0]
    groups = lax.axis_size("loans")
    me_loan = lax.axis_index("loans")
    covar = jnp.dot(loan_features, hazard_coef, preferred_element_type=jnp.float32)
    piece = lax.all_gather(region_hpi, "loans", axis=0, tiled=True)
    rows = piece.shape[0]
    marks = (loan_region[None, :] == lax.iota(jnp.int32, rows)[:, None]).astype(jnp.float32)
    loan_hpi = jnp.einsum("rc,rl->cl", piece.reshape(rows, -1), marks, precision=highest)
    loan_hpi = loan_hpi.reshape(steps, paths_here, loans_here)
    rate_month = coupon / 12.0
    term_left = (loan_term - loan_age).astype(jnp.float32)
    held = jnp.broadcast_to(balance[None, :], (paths_here, loans_here))
    prin_list = []
    int_list = []
    for step in range(steps):
        sched_rate = rate_month / jnp.expm1((term_left - step) * jnp.log1p(rate_month))
        held, principal, interest = loan_month(
            held, covar, coupon, rate_month, sched_rate, rate_paths[1, step], loan_hpi[step]
        )
        prin_list.append(principal)
        int_list.append(interest)
    cash = jnp.stack([jnp.stack(prin_list, 1), jnp.stack(int_list, 1)], 1)
    deal_ids = lax.iota(jnp.int32, deals)
    match = loan_deal[:, None] == deal_ids[None, :]
    onehot_deal = match.astype(jnp.float32)
    totals = lax.psum(jnp.dot(balance, onehot_deal, precision=highest), "loans")
    owners = deal_owner[:, 0]
    order_key = owners * deals + deal_ids
    position = jnp.sum((order_key[None, :] < order_key[:, None]).astype(jnp.int32), axis=1)
    place = (position[None, :] == deal_ids[:, None]).astype(jnp.float32)
    ahead_mask = priority_mask(tranche_order)
    portion = paths_here // groups
    block = cash.reshape(-1, loans_here)
    path_flows = lax.psum_scatter(
        jnp.dot(block, onehot_deal, precision=highest).reshape(
            portion * lax.axis_size("loans"), 2, steps, deals
        ),
        "loans",
        scatter_dimension=0,
        tiled=True,
    )
    flows = path_flows.transpose(3, 0, 1, 2)
    short = lax.dynamic_slice_in_dim(rate_paths[0], me_loan * portion, portion, 1)
    by_deal = waterfall(
        flows[:, :, 0, :],
        flows[:, :, 1, :],
        totals,
        tranche_share,
        tranche_rate,
        ahead_mask,
        short,
        jnp.ones((deals,), jnp.float32),
    )
    ordered = jnp.dot(place, by_deal, precision=highest)
    mine = lax.psum(ordered, "loans")
    total = lax.psum(mine, "paths")
    all_paths = paths_here * lax.axis_size("paths")
    return 100.0 * (total / all_paths - 1.0)


MESH = pl.DeviceIdType.MESH


def rows_of(x):
    return x.reshape((1,) + x.shape)


def pool_kernel(groups, lanes_out, *refs):
    n_loans, n_paths = groups
    sources, out = refs[:14], refs[14]
    feat, coef, coupon, balance, term, age, region, deal, hpi, rates, owner, order, share, trate = refs[15:29]
    (loan_tx, loan_rx, early_tx, early_rx, late_tx, late_rx, early_tab, late_tab, mort, terms, late_stay, members, balances,
     early_cash, late_cash, early_sums, late_sums, early_a, early_b, late_a, late_b, fracs, falls, worth, table, cols, part, part_rx,
     in_sem, loan_ss, loan_rs, pass_ss, pass_rs, early_ss, early_rs, late_ss, late_rs, part_ss, part_rs) = refs[29:]
    f32, bf16 = jnp.float32, jnp.bfloat16
    me = lax.axis_index("loans")
    me_path = lax.axis_index("paths")
    rank = me * n_paths + me_path
    n_all = n_loans * n_paths
    n = coupon.shape[1]
    steps, rows, paths = hpi.shape
    here = paths // n_loans
    early = n_loans
    late = steps - early
    split = late_tx.shape[1]
    deals, tranches = share.shape
    copies = lanes_out // deals
    halves = n // n_paths // 128

    def other(off):
        there = lax.rem(rank + off, n_all)
        return {"loans": there // n_paths, "paths": lax.rem(there, n_paths)}

    barrier = pltpu.get_barrier_semaphore()
    loads = [pltpu.make_async_copy(a, b, in_sem.at[k]) for k, (a, b) in enumerate(zip(sources, refs[15:29]))]
    for off in range(1, n_loans):
        pl.semaphore_signal(barrier, inc=1, device_id={"loans": lax.rem(me + off, n_loans)}, device_id_type=MESH)
    for off in range(1, n_paths):
        pl.semaphore_signal(barrier, inc=1, device_id={"paths": lax.rem(me_path + off, n_paths)}, device_id_type=MESH)
    first = (0, 8, 1, 2, 3, 4, 5, 6, 7)
    for k in first + tuple(range(9, 14)):
        loads[k].start()
    for k in first:
        if k != 8:
            loads[k].wait()

    covar = lax.dot_general(coef[...], feat[...], (((1,), (1,)), ((), ())), preferred_element_type=f32)
    note = coupon[...]
    home = jnp.zeros((1, n), jnp.int32)
    for k in range(1, n_loans):
        home = home + jnp.where(region[...] >= k * rows, 1, 0)
    bundle = jnp.concatenate(
        [
            0.5 * (covar[0:1, :] + prepay_base + incentive * note),
            0.5 * (covar[1:2, :] + default_base),
            note / 12.0,
            balance[...],
            (term[...] - age[...]).astype(f32),
            (region[...] - home * rows).astype(f32),
            deal[...].astype(f32),
            home.astype(f32),
        ],
        axis=0,
    )
    for q in range(n_paths):
        for k in range(halves):
            at = (q * halves + k) * 128
            loan_tx[q, k] = bundle[:, at:at + 128]

    loads[8].wait()

    def turn(blocks):
        quarter = lax.broadcasted_iota(jnp.int32, blocks[0].shape, 1) // here
        half, odd = quarter < 2, quarter % 2 == 1
        swapped = [pltpu.roll(x, 2 * here, 1) for x in blocks]
        blocks = ([jnp.where(half, blocks[t], swapped[t + 2]) for t in range(2)]
                  + [jnp.where(half, swapped[t], blocks[t + 2]) for t in range(2)])
        turned = []
        for t in (0, 2):
            turned.append(jnp.where(odd, pltpu.roll(blocks[t + 1], here, 1), blocks[t]))
            turned.append(jnp.where(odd, blocks[t + 1], pltpu.roll(blocks[t], paths - here, 1)))
        return turned

    for q, block in enumerate(turn([hpi[t] for t in range(early)])):
        early_tx[q] = block
    loan_copies, pass_copies, early_copies, late_copies = [], [], [], []
    for off in range(1, n_loans):
        there, source = lax.rem(me + off, n_loans), lax.rem(me + n_loans - off, n_loans)
        loan_copies.append(pltpu.make_async_remote_copy(
            src_ref=loan_tx.at[me_path], dst_ref=loan_rx.at[rank], send_sem=loan_ss.at[off],
            recv_sem=loan_rs.at[off], device_id={"loans": there}, device_id_type=MESH))
        slot = source * n_paths + me_path
        for hop in range(1, n_paths):
            pass_copies.append(pltpu.make_async_remote_copy(
                src_ref=loan_rx.at[slot], dst_ref=loan_rx.at[slot],
                send_sem=pass_ss.at[off, hop], recv_sem=pass_rs.at[off, hop],
                device_id={"paths": lax.rem(me_path + hop, n_paths)}, device_id_type=MESH))
        early_copies.append(pltpu.make_async_remote_copy(
            src_ref=early_tx.at[there], dst_ref=early_rx.at[me], send_sem=early_ss.at[off],
            recv_sem=early_rs.at[off], device_id={"loans": there}, device_id_type=MESH))
        late_copies.append(pltpu.make_async_remote_copy(
            src_ref=late_tx.at[there], dst_ref=late_rx.at[me], send_sem=late_ss.at[off],
            recv_sem=late_rs.at[off], device_id={"loans": there}, device_id_type=MESH))
    pl.semaphore_wait(barrier, n_loans + n_paths - 2)
    for copy in loan_copies:
        copy.start()
    for copy in early_copies:
        copy.start()
    pad = jnp.zeros((2 * split - rows, paths), f32)
    blocks = [hpi[early + t, 0:split, :] for t in range(late)]
    blocks += [jnp.concatenate([hpi[early + t, split:rows, :], pad], axis=0) for t in range(late)]
    for q, block in enumerate(turn(blocks)):
        late_tx[q] = block
    for copy in late_copies:
        copy.start()
    early_rx[me] = early_tx[me]
    late_rx[me] = late_tx[me]
    for q in range(n_paths):
        loan_rx[me * n_paths + q] = loan_tx[q]

    for k in range(9, 14):
        loads[k].wait()
    key = (jnp.broadcast_to(owner[...], (deals, deals)) * deals
           + lax.broadcasted_iota(jnp.int32, (deals, deals), 1)).astype(f32)
    key_col = jnp.concatenate([key, jnp.zeros((128 - deals, deals), f32)], axis=0).T[:, :deals]
    below = jnp.where(key_col < key, 1.0, 0.0).astype(f32)
    spot = jnp.sum(below, axis=0, keepdims=True)
    perm = jnp.where(spot == lax.broadcasted_iota(jnp.int32, (deals, deals), 0).astype(f32), 1.0, 0.0).astype(f32)
    listing = jnp.sum(perm * lax.broadcasted_iota(jnp.int32, (deals, deals), 1).astype(f32), axis=1, keepdims=True)

    def spread(x):
        x = jnp.dot(perm, x, preferred_element_type=f32, precision=lax.Precision.HIGHEST)
        x = jnp.concatenate([x, jnp.zeros((deals, 128 - tranches), f32)], axis=1)
        return jnp.concatenate([x] * copies, axis=0).T[:tranches, :]

    table[...] = spread(order[...].astype(f32))
    share_t = spread(share[...])
    rate_t = spread(trate[...])
    names = lax.broadcasted_iota(jnp.int32, (tranches, lanes_out), 0).astype(f32)

    def walk(j, carry):
        run, upto = carry
        hit = names == table[pl.ds(j, 1), :]
        run = run + jnp.sum(jnp.where(hit, share_t, 0.0), axis=0, keepdims=True)
        return run, jnp.where(hit, run, upto)

    whole, upto = lax.fori_loop(
        0, tranches, walk, (jnp.zeros((1, lanes_out), f32), jnp.zeros((tranches, lanes_out), f32)), unroll=4)
    weight = share_t / whole
    upto = upto / whole
    per_weight = 1.0 / weight
    falls[0], falls[1], falls[2], falls[3] = upto, per_weight, rate_t * weight, rate_t

    stack = jnp.concatenate([rates[t] for t in range(steps)] + [jnp.zeros((128 - 2 * steps, paths), f32)], axis=0)
    cols[...] = stack.T
    mine = cols[pl.ds(pl.multiple_of(me * here, here), here), :]
    disc = []
    total = jnp.zeros((here, 1), f32)
    for t in range(steps):
        mort[t] = jnp.broadcast_to((0.5 * incentive) * mine[:, 2 * t + 1:2 * t + 2], (here, 128))
        total = total + (mine[:, 2 * t:2 * t + 1] + oas_spread)
        disc.append(jnp.exp(-total / 12.0))

    for k, copy in enumerate(loan_copies):
        copy.wait_recv()
        for again in pass_copies[k * (n_paths - 1):(k + 1) * (n_paths - 1)]:
            again.start()
    for copy in pass_copies:
        copy.wait_recv()

    ages = lax.broadcasted_iota(jnp.int32, (8, 128), 0).astype(f32)
    listed = jnp.broadcast_to(listing, (deals, 128))

    def prepare(i, carry):
        for k in range(halves):
            lv = loan_rx[i, k]
            r = lv[2:3, :]
            grown = 1.0 + r
            log = jnp.log(grown) * (r / (grown - 1.0))
            x = (lv[4:5, :] - ages) * log
            terms[i, k] = 1.0 - (2.0 * r) / (jnp.exp(x) - 1.0)
            hit = listed == lv[6:7, :]
            high = r.astype(bf16).astype(f32)
            member = jnp.concatenate(
                [jnp.where(hit, 1.0, 0.0), jnp.where(hit, high, 0.0), jnp.where(hit, r - high, 0.0),
                 jnp.zeros((lanes_out - 3 * deals, 128), f32)], axis=0).astype(bf16)
            members[i * halves + k] = member
            for t in range(late):
                late_stay[i, k, t * here:(t + 1) * here, :] = 1.0 - jnp.tanh(lv[0:1, :] - mort[early + t])
        return carry

    lax.fori_loop(0, n_all, prepare, 0, unroll=PREPARE)
    step_scale = -0.5 * price_sens / (fixed_point * 65536.0)

    def pairs(x):
        x = jnp.floor(x * fixed_point + 0.5).astype(jnp.int32)
        return [(x[t * here:(t + 1) * here] << 16) | (x[(t + 1) * here:(t + 2) * here] & 65535)
                for t in range(0, x.shape[0] // here, 2)]

    def months(start, count, tab, cash, acc, found_a, found_b, span):
        height = count * here
        cash[0] = jnp.zeros(cash.shape[1:], bf16)
        acc[...] = jnp.zeros_like(acc)

        sets = n_all // span
        each = span * halves

        def deal_sums(i):
            flat = jnp.concatenate([cash[i, g] for g in range(each)], axis=1)
            base = jnp.maximum(i - 1, 0) * each
            those = jnp.concatenate([members[base + g] for g in range(each)], axis=1)
            return lax.dot_general(flat, those, (((1,), (1,)), ((), ())), preferred_element_type=f32)

        def row(ref, s, k, j):
            return jnp.broadcast_to(ref[s, k, j:j + 1, :], (8, 128))

        def look_up(i, found):
            for g in range(each):
                s, k = i * span + g // halves, g % halves
                lane = row(loan_rx, s, k, 5).astype(jnp.int32)
                home = row(loan_rx, s, k, 7)
                away = [home == float(c) for c in range(1, n_loans)]
                for low in range(0, height // 2, 8):
                    v = None
                    for c in range(n_loans):
                        x = jnp.take_along_axis(tab[c, low:low + 8, :], lane, axis=1, mode="promise_in_bounds")
                        v = x if v is None else jnp.where(away[c - 1], x, v)
                    found[g, low:low + 8, :] = v

        def advance(i, found):
            acc[...] += deal_sums(i)
            for g in range(each):
                s, k = i * span + g // halves, g % halves
                for p in range(0, here, 16):
                    duo = [[], []]
                    for b in range(2):
                        at = p + 8 * b
                        held = row(loan_rx, s, k, 3) if start == 0 else balances[s, k, at:at + 8, :]
                        for two in range(0, count, 2):
                            low = (two // 2) * here + at
                            v = found[g, low:low + 8, :]
                            for t, x in ((two, v & -65536), (two + 1, v << 16)):
                                if start == 0:
                                    stay = 1.0 - jnp.tanh(row(loan_rx, s, k, 0) - mort[t, at:at + 8, :])
                                else:
                                    stay = late_stay[s, k, t * here + at:t * here + at + 8, :]
                                alive = row(terms, s, k, start + t) - jnp.tanh(
                                    row(loan_rx, s, k, 1) + x.astype(f32) * step_scale)
                                held = held * (stay * alive)
                                duo[b].append(held)
                        if start + count < steps:
                            balances[s, k, at:at + 8, :] = held
                    for t in range(count):
                        x = jnp.concatenate([duo[0][t], duo[1][t]], axis=0)
                        high = x.astype(bf16)
                        cash[i + 1, g, t * here + p:t * here + p + 16, :] = high
                        cash[i + 1, g, height + t * here + p:height + t * here + p + 16, :] = (
                            x - high.astype(f32)).astype(bf16)

                if start == 0:
                    x = row(loan_rx, s, k, 3)
                    high = x.astype(bf16).astype(f32)
                    cash[i + 1, g, 2 * height:, :] = jnp.concatenate([high, x - high], axis=0).astype(bf16)

        def two_sets(m, carry):
            look_up(2 * m + 1, found_b)
            advance(2 * m, found_a)
            look_up(2 * m + 2, found_a)
            advance(2 * m + 1, found_b)
            return carry

        look_up(0, found_a)
        lax.fori_loop(0, sets // 2 - 1, two_sets, 0)
        look_up(sets - 1, found_b)
        advance(sets - 2, found_a)
        advance(sets - 1, found_b)
        sums = acc[...] + deal_sums(sets)
        first = sums[2 * height:2 * height + 8] + sums[2 * height + 8:] if start == 0 else None
        sums = sums[:height] + sums[height:2 * height]
        return first, [sums[t * here:(t + 1) * here] * (0.25 ** (start + t + 1)) for t in range(count)]

    sub = here // copies
    group_of = lax.broadcasted_iota(jnp.int32, (sub, lanes_out), 1) // deals

    def packed(x):
        x = jnp.broadcast_to(x, (here, lanes_out))
        y = x[0:sub]
        for c in range(1, copies):
            y = jnp.where(group_of == c, x[c * sub:(c + 1) * sub], y)
        return y

    def shifted(x, column):
        pieces = [x[c * sub:(c + 1) * sub] for c in range(copies)]
        turned = [pltpu.roll(y, ((c - column) % copies) * deals, 1) if (c - column) % copies else y
                  for c, y in enumerate(pieces)]
        y = turned[0]
        for c in range(1, copies):
            y = jnp.where(group_of == c, turned[c], y)
        return y

    fall = [packed(disc[t]) for t in range(steps)]

    def flows(state, sums):
        held, inter, paid_upto = state
        gone, gains = [], []
        for x in sums:
            after = shifted(x, 0)
            paid_upto = paid_upto + jnp.maximum(held - after, 0.0)
            gone.append(paid_upto * per_start)
            gains.append(inter * per_start)
            held, inter = after, shifted(x, 1) + shifted(x, 2)
        return (held, inter, paid_upto), gone, gains

    def line(j, k):
        return jnp.broadcast_to(falls[j, k:k + 1, :], (sub, lanes_out))

    def left_over(k, gone):
        return jnp.clip((line(0, k) - gone) * line(1, k), 0.0, 1.0)

    def settle(first, gone, d, extra):
        dues = [jnp.zeros((sub, lanes_out), f32) for _ in range(4)]
        for k in range(tranches):
            frac = 1.0 if first else fracs[k]
            later = left_over(k, gone)
            w = (frac - later) * d + (line(3, k) * frac) * extra
            worth[k] = w if first else worth[k] + w
            dues[k % 4] = dues[k % 4] + line(2, k) * later
            fracs[k] = later
        return (dues[0] + dues[1]) + (dues[2] + dues[3])

    for copy in early_copies:
        copy.wait_recv()
    tail = jnp.zeros((128 - rows, paths), f32)
    for c in range(n_loans):
        for k, x in enumerate(pairs(jnp.concatenate([early_rx[c], tail], axis=0).T)):
            early_tab[c, k * here:(k + 1) * here, :] = x
    bases, sums = months(0, early, early_tab, early_cash, early_sums, early_a, early_b, EARLY_SPAN)
    bases = jnp.concatenate([bases[:sub]] * copies, axis=0)
    per_start = 1.0 / shifted(bases, 0)
    for copy in late_copies:
        copy.wait_recv()
    lower = late * here
    for c in range(n_loans):
        x = jnp.concatenate([late_rx[c], jnp.zeros((128 - split, paths), f32)], axis=0).T
        upper = pltpu.roll(x[lower:], split, 1)
        late_tab[c] = pairs(jnp.where(lax.broadcasted_iota(jnp.int32, (lower, 128), 1) < split, x[:lower], upper))[0]
    state = (shifted(bases, 0), shifted(bases, 1) + shifted(bases, 2), jnp.zeros((sub, lanes_out), f32))
    state, gone, gains = flows(state, sums)
    dues = jnp.sum(falls[2], axis=0, keepdims=True)
    for t in range(early):
        dues = settle(t == 0, gone[t], fall[t], gains[t] * fall[t] / dues)
    extra = (state[1] * per_start) * fall[early] / dues
    for k in range(tranches):
        worth[k] = worth[k] + fracs[k] * (fall[early] + line(3, k) * extra)

    _, late_totals = months(early, late, late_tab, late_cash, late_sums, late_a, late_b, LATE_SPAN)
    state, gone, gains = flows(state, late_totals)
    dues = [jnp.zeros((sub, lanes_out), f32) for _ in range(4)]
    for k in range(tranches):
        later = left_over(k, gone[0])
        dues[k % 4] = dues[k % 4] + line(2, k) * later
        fracs[k] = later
    extra = gains[1] * fall[steps - 1] / ((dues[0] + dues[1]) + (dues[2] + dues[3]))
    total = []
    for k in range(tranches):
        frac = fracs[k]
        later = left_over(k, gone[1])
        w = (worth[k] - frac * fall[early] + (frac - later) * fall[steps - 1]
             + (line(3, k) * frac) * extra + later * fall[steps - 1])
        total.append(jnp.sum(w, axis=0, keepdims=True))

    wt = jnp.concatenate(total + [jnp.zeros((128 - tranches, lanes_out), f32)], axis=0).T
    acc = wt[0:deals]
    low = lax.broadcasted_iota(jnp.int32, (deals // 2, 128), 1) < 64
    for c in range(1, copies):
        acc = acc + wt[c * deals:(c + 1) * deals]
    acc = jnp.where(low, acc[:deals // 2], pltpu.roll(acc[deals // 2:], 64, 1))
    part[...] = acc
    part_copies = []
    for off in range(1, n_all):
        part_copies.append(pltpu.make_async_remote_copy(
            src_ref=part, dst_ref=part_rx.at[rank], send_sem=part_ss.at[off], recv_sem=part_rs.at[off],
            device_id=other(off), device_id_type=MESH))
    for copy in part_copies:
        copy.start()
    part_rx[rank] = acc
    for copy in part_copies:
        copy.wait_recv()
    acc = part_rx[0]
    for k in range(1, n_all):
        acc = acc + part_rx[k]
    acc = 100.0 * (acc / (paths * n_paths) - 1.0)
    out[:deals // 2, :] = acc[:, :tranches]
    out[deals // 2:, :] = pltpu.roll(acc, 64, 1)[:, :tranches]
    for copy in loan_copies + pass_copies + early_copies + late_copies + part_copies:
        copy.wait_send()


def fused(loan_features, hazard_coef, coupon, balance, loan_term, loan_age, loan_region, loan_deal,
          region_hpi, rate_paths, deal_owner, tranche_order, tranche_share, tranche_rate):
    n_loans, n_paths = lax.axis_size("loans"), lax.axis_size("paths")
    n = coupon.shape[0]
    rows, steps, paths = region_hpi.shape
    deals, tranches = tranche_share.shape
    here = paths // n_loans
    lanes_out = 128
    split = -(-rows // 16) * 8
    early, late = n_loans, steps - n_loans
    halves = n // n_paths // 128
    n_all = n_loans * n_paths
    f32, bf16 = jnp.float32, jnp.bfloat16
    dma = pltpu.SemaphoreType.DMA
    operands = (loan_features, hazard_coef.T, rows_of(coupon), rows_of(balance), rows_of(loan_term), rows_of(loan_age),
                rows_of(loan_region), rows_of(loan_deal), region_hpi.transpose(1, 0, 2),
                rate_paths.transpose(1, 0, 2), deal_owner.reshape(1, deals), tranche_order, tranche_share, tranche_rate)
    return pl.pallas_call(
        functools.partial(pool_kernel, (n_loans, n_paths), lanes_out),
        out_shape=pltpu.VMEM((deals, tranches), f32),
        in_specs=[pl.BlockSpec(memory_space=pl.ANY)] * len(operands),
        out_specs=pl.BlockSpec(memory_space=pltpu.VMEM),
        scratch_shapes=[pltpu.VMEM(x.shape, x.dtype) for x in operands] + [
            pltpu.VMEM((n_paths, halves, 8, 128), f32),
            pltpu.VMEM((n_all, halves, 8, 128), f32),
            pltpu.VMEM((n_loans, rows, paths), f32),
            pltpu.VMEM((n_loans, rows, paths), f32),
            pltpu.VMEM((n_loans, split, paths), f32),
            pltpu.VMEM((n_loans, split, paths), f32),
            pltpu.VMEM((n_loans, early // 2 * here, 128), jnp.int32),
            pltpu.VMEM((n_loans, late // 2 * here, 128), jnp.int32),
            pltpu.VMEM((steps, here, 128), f32),
            pltpu.VMEM((n_all, halves, 8, 128), f32),
            pltpu.VMEM((n_all, halves, late * here, 128), f32),
            pltpu.VMEM((n_all * halves, lanes_out, 128), bf16),
            pltpu.VMEM((n_all, halves, here, 128), f32),
            pltpu.VMEM((n_all // EARLY_SPAN + 1, EARLY_SPAN * halves, 2 * early * here + 16, 128), bf16),
            pltpu.VMEM((n_all // LATE_SPAN + 1, LATE_SPAN * halves, 2 * late * here, 128), bf16),
            pltpu.VMEM((2 * early * here + 16, lanes_out), f32),
            pltpu.VMEM((2 * late * here, lanes_out), f32),
            pltpu.VMEM((EARLY_SPAN * halves, early // 2 * here, 128), jnp.int32),
            pltpu.VMEM((EARLY_SPAN * halves, early // 2 * here, 128), jnp.int32),
            pltpu.VMEM((LATE_SPAN * halves, late // 2 * here, 128), jnp.int32),
            pltpu.VMEM((LATE_SPAN * halves, late // 2 * here, 128), jnp.int32),
            pltpu.VMEM((tranches, here * deals // lanes_out, lanes_out), f32),
            pltpu.VMEM((4, tranches, lanes_out), f32),
            pltpu.VMEM((tranches, here * deals // lanes_out, lanes_out), f32),
            pltpu.VMEM((tranches, lanes_out), f32),
            pltpu.VMEM((paths, 128), f32),
            pltpu.VMEM((deals // 2, 128), f32),
            pltpu.VMEM((n_all, deals // 2, 128), f32),
            dma((len(operands),)),
            dma((n_loans,)), dma((n_loans,)), dma((n_loans, n_paths)), dma((n_loans, n_paths)),
            dma((n_loans,)), dma((n_loans,)), dma((n_loans,)), dma((n_loans,)),
            dma((n_all,)), dma((n_all,)),
        ],
        compiler_params=pltpu.CompilerParams(collective_id=0, has_side_effects=True),
    )(*operands)


def fits(args):
    n = args[2].shape[0]
    paths = args[8].shape[2]
    deals, tranches = args[12].shape
    n_loans = lax.axis_size("loans")
    rows, steps = args[8].shape[:2]
    return (
        paths == 128 and n_loans == 4 and 2 * (steps - n_loans) == n_loans and rows % 8 == 0 and 64 < rows <= 128
        and deals in (16, 32) and tranches == 64
        and (paths // n_loans) % (8 * (128 // deals)) == 0
        and n % (128 * lax.axis_size("paths")) == 0 and n <= 2048
    )


def device_program(*args):
    return fused(*args) if fits(args) else on_device(*args)


def solution(mesh):
    in_specs = (
        P(("groups", "loans"), None),
        P(),
        P(("groups", "loans")),
        P(("groups", "loans")),
        P(("groups", "loans")),
        P(("groups", "loans")),
        P(("groups", "loans")),
        P(("groups", "loans")),
        P(("groups", "loans"), None, "paths"),
        P(None, None, ("groups", "paths")),
        P("groups", None),
        P("groups", None),
        P("groups", None),
        P("groups", None),
    )
    out_specs = P("groups", None)
    return jax.shard_map(
        device_program, mesh=mesh, in_specs=in_specs, out_specs=out_specs, check_vma=False
    )
```

```python
import functools

import jax
import jax.numpy as jnp
from jax import lax
from jax.experimental import pallas as pl
from jax.experimental.pallas import tpu as pltpu
from jax.sharding import PartitionSpec as P

prepay_base = -4.0
incentive = 40.0
default_base = -6.0
price_sens = 12.0
oas_spread = 0.005
fixed_point = 54000.0
PREPARE = 4
EARLY_SPAN = 4
LATE_SPAN = 4


def loan_month(held, covar, coupon, rate_month, sched_rate, mortgage_now, hpi_now):
    smm = jax.nn.sigmoid(
        covar[:, 0][None, :] + prepay_base + incentive * (coupon[None, :] - mortgage_now[:, None])
    )
    mdr = jax.nn.sigmoid(covar[:, 1][None, :] + default_base - price_sens * hpi_now)
    interest = held * rate_month[None, :]
    sched = held * sched_rate[None, :]
    lost = mdr * held
    prepaid = smm * (held - sched - lost)
    principal = sched + prepaid + lost
    return (held - principal, principal, interest)


def priority_mask(tranche_order):
    count = tranche_order.shape[1]
    spots = jnp.arange(count, dtype=jnp.int32)
    hits = tranche_order[:, :, None] == spots[None, None, :]
    prio = jnp.sum(jnp.where(hits, spots[None, :, None], 0), axis=1)
    return (prio[:, :, None] < prio[:, None, :]).astype(jnp.float32)


def waterfall(princ, inter, starts, shares, rates, ahead_mask, short, valid):
    steps = princ.shape[2]
    blank = 1.0 - valid
    weights = shares / (jnp.sum(shares, axis=1, keepdims=True) + blank[:, None])
    opening = weights * starts[:, None]
    safe_open = opening + blank[:, None]
    held = jnp.broadcast_to(opening[:, None, :], (princ.shape[0], princ.shape[1], shares.shape[1]))
    decay = []
    run = jnp.zeros_like(short[0])
    for step in range(steps):
        run = run + (short[step] + oas_spread)
        decay.append(jnp.exp(-run / 12.0))
    worth = jnp.zeros_like(held)
    for step in range(steps):
        ahead = jnp.einsum("xpj,xjk->xpk", held, ahead_mask, precision=lax.Precision.HIGHEST)
        paid = jnp.minimum(jnp.maximum(princ[:, :, step, None] - ahead, 0.0), held)
        coupon_due = rates[:, None, :] * held
        denom = jnp.sum(coupon_due, axis=2, keepdims=True) + blank[:, None, None]
        flow = paid + inter[:, :, step, None] * coupon_due / denom
        worth = worth + flow * decay[step][None, :, None]
        held = held - paid
    worth = worth + held * decay[steps - 1][None, :, None]
    return jnp.sum(worth / safe_open[:, None, :], axis=1)


def on_device(
    loan_features,
    hazard_coef,
    coupon,
    balance,
    loan_term,
    loan_age,
    loan_region,
    loan_deal,
    region_hpi,
    rate_paths,
    deal_owner,
    tranche_order,
    tranche_share,
    tranche_rate,
):
    highest = lax.Precision.HIGHEST
    loans_here = coupon.shape[0]
    paths_here = rate_paths.shape[2]
    steps = rate_paths.shape[1]
    deals = deal_owner.shape[0]
    groups = lax.axis_size("loans")
    me_loan = lax.axis_index("loans")
    covar = jnp.dot(loan_features, hazard_coef, preferred_element_type=jnp.float32)
    piece = lax.all_gather(region_hpi, "loans", axis=0, tiled=True)
    rows = piece.shape[0]
    marks = (loan_region[None, :] == lax.iota(jnp.int32, rows)[:, None]).astype(jnp.float32)
    loan_hpi = jnp.einsum("rc,rl->cl", piece.reshape(rows, -1), marks, precision=highest)
    loan_hpi = loan_hpi.reshape(steps, paths_here, loans_here)
    rate_month = coupon / 12.0
    term_left = (loan_term - loan_age).astype(jnp.float32)
    held = jnp.broadcast_to(balance[None, :], (paths_here, loans_here))
    prin_list = []
    int_list = []
    for step in range(steps):
        sched_rate = rate_month / jnp.expm1((term_left - step) * jnp.log1p(rate_month))
        held, principal, interest = loan_month(
            held, covar, coupon, rate_month, sched_rate, rate_paths[1, step], loan_hpi[step]
        )
        prin_list.append(principal)
        int_list.append(interest)
    cash = jnp.stack([jnp.stack(prin_list, 1), jnp.stack(int_list, 1)], 1)
    deal_ids = lax.iota(jnp.int32, deals)
    match = loan_deal[:, None] == deal_ids[None, :]
    onehot_deal = match.astype(jnp.float32)
    totals = lax.psum(jnp.dot(balance, onehot_deal, precision=highest), "loans")
    owners = deal_owner[:, 0]
    order_key = owners * deals + deal_ids
    position = jnp.sum((order_key[None, :] < order_key[:, None]).astype(jnp.int32), axis=1)
    place = (position[None, :] == deal_ids[:, None]).astype(jnp.float32)
    ahead_mask = priority_mask(tranche_order)
    portion = paths_here // groups
    block = cash.reshape(-1, loans_here)
    path_flows = lax.psum_scatter(
        jnp.dot(block, onehot_deal, precision=highest).reshape(
            portion * lax.axis_size("loans"), 2, steps, deals
        ),
        "loans",
        scatter_dimension=0,
        tiled=True,
    )
    flows = path_flows.transpose(3, 0, 1, 2)
    short = lax.dynamic_slice_in_dim(rate_paths[0], me_loan * portion, portion, 1)
    by_deal = waterfall(
        flows[:, :, 0, :],
        flows[:, :, 1, :],
        totals,
        tranche_share,
        tranche_rate,
        ahead_mask,
        short,
        jnp.ones((deals,), jnp.float32),
    )
    ordered = jnp.dot(place, by_deal, precision=highest)
    mine = lax.psum(ordered, "loans")
    total = lax.psum(mine, "paths")
    all_paths = paths_here * lax.axis_size("paths")
    return 100.0 * (total / all_paths - 1.0)


MESH = pl.DeviceIdType.MESH


def rows_of(x):
    return x.reshape((1,) + x.shape)


def pool_kernel(groups, lanes_out, *refs):
    n_loans, n_paths = groups
    sources, out = refs[:14], refs[14]
    feat, coef, coupon, balance, term, age, region, deal, hpi, rates, owner, order, share, trate = refs[15:29]
    (loan_tx, loan_rx, early_tx, early_rx, late_tx, late_rx, early_tab, late_tab, mort, terms, late_stay, members, balances,
     early_cash, late_cash, early_sums, late_sums, early_a, early_b, late_a, late_b, fracs, falls, worth, table, cols, part, part_rx,
     in_sem, loan_ss, loan_rs, pass_ss, pass_rs, early_ss, early_rs, late_ss, late_rs, part_ss, part_rs) = refs[29:]
    f32, bf16 = jnp.float32, jnp.bfloat16
    me = lax.axis_index("loans")
    me_path = lax.axis_index("paths")
    rank = me * n_paths + me_path
    n_all = n_loans * n_paths
    n = coupon.shape[1]
    steps, rows, paths = hpi.shape
    here = paths // n_loans
    early = n_loans
    late = steps - early
    split = late_tx.shape[1]
    deals, tranches = share.shape
    copies = lanes_out // deals
    halves = n // n_paths // 128

    def other(off):
        there = lax.rem(rank + off, n_all)
        return {"loans": there // n_paths, "paths": lax.rem(there, n_paths)}

    barrier = pltpu.get_barrier_semaphore()
    loads = [pltpu.make_async_copy(a, b, in_sem.at[k]) for k, (a, b) in enumerate(zip(sources, refs[15:29]))]
    for off in range(1, n_loans):
        pl.semaphore_signal(barrier, inc=1, device_id={"loans": lax.rem(me + off, n_loans)}, device_id_type=MESH)
    for off in range(1, n_paths):
        pl.semaphore_signal(barrier, inc=1, device_id={"paths": lax.rem(me_path + off, n_paths)}, device_id_type=MESH)
    first = (0, 8, 1, 2, 3, 4, 5, 6, 7)
    for k in first + tuple(range(9, 14)):
        loads[k].start()
    for k in first:
        if k != 8:
            loads[k].wait()

    covar = lax.dot_general(coef[...], feat[...], (((1,), (1,)), ((), ())), preferred_element_type=f32)
    note = coupon[...]
    home = jnp.zeros((1, n), jnp.int32)
    for k in range(1, n_loans):
        home = home + jnp.where(region[...] >= k * rows, 1, 0)
    bundle = jnp.concatenate(
        [
            0.5 * (covar[0:1, :] + prepay_base + incentive * note),
            0.5 * (covar[1:2, :] + default_base),
            note / 12.0,
            balance[...],
            (term[...] - age[...]).astype(f32),
            (region[...] - home * rows).astype(f32),
            deal[...].astype(f32),
            home.astype(f32),
        ],
        axis=0,
    )
    for q in range(n_paths):
        for k in range(halves):
            at = (q * halves + k) * 128
            loan_tx[q, k] = bundle[:, at:at + 128]

    loads[8].wait()

    def turn(blocks):
        quarter = lax.broadcasted_iota(jnp.int32, blocks[0].shape, 1) // here
        half, odd = quarter < 2, quarter % 2 == 1
        swapped = [pltpu.roll(x, 2 * here, 1) for x in blocks]
        blocks = ([jnp.where(half, blocks[t], swapped[t + 2]) for t in range(2)]
                  + [jnp.where(half, swapped[t], blocks[t + 2]) for t in range(2)])
        turned = []
        for t in (0, 2):
            turned.append(jnp.where(odd, pltpu.roll(blocks[t + 1], here, 1), blocks[t]))
            turned.append(jnp.where(odd, blocks[t + 1], pltpu.roll(blocks[t], paths - here, 1)))
        return turned

    for q, block in enumerate(turn([hpi[t] for t in range(early)])):
        early_tx[q] = block
    loan_copies, pass_copies, early_copies, late_copies = [], [], [], []
    for off in (1, 2, 3):
        there = source = (me + 1 - 2 * lax.rem(me, 2), lax.rem(me + 2, n_loans), n_loans - 1 - me)[off - 1]
        loan_copies.append(pltpu.make_async_remote_copy(
            src_ref=loan_tx.at[me_path], dst_ref=loan_rx.at[rank], send_sem=loan_ss.at[off],
            recv_sem=loan_rs.at[off], device_id={"loans": there}, device_id_type=MESH))
        slot = source * n_paths + me_path
        for hop in range(1, n_paths):
            pass_copies.append(pltpu.make_async_remote_copy(
                src_ref=loan_rx.at[slot], dst_ref=loan_rx.at[slot],
                send_sem=pass_ss.at[off, hop], recv_sem=pass_rs.at[off, hop],
                device_id={"paths": lax.rem(me_path + hop, n_paths)}, device_id_type=MESH))
        early_copies.append(pltpu.make_async_remote_copy(
            src_ref=early_tx.at[there], dst_ref=early_rx.at[me], send_sem=early_ss.at[off],
            recv_sem=early_rs.at[off], device_id={"loans": there}, device_id_type=MESH))
        late_copies.append(pltpu.make_async_remote_copy(
            src_ref=late_tx.at[there], dst_ref=late_rx.at[me], send_sem=late_ss.at[off],
            recv_sem=late_rs.at[off], device_id={"loans": there}, device_id_type=MESH))
    pl.semaphore_wait(barrier, n_loans + n_paths - 2)
    for copy in loan_copies:
        copy.start()
    for copy in early_copies:
        copy.start()
    pad = jnp.zeros((2 * split - rows, paths), f32)
    blocks = [hpi[early + t, 0:split, :] for t in range(late)]
    blocks += [jnp.concatenate([hpi[early + t, split:rows, :], pad], axis=0) for t in range(late)]
    for q, block in enumerate(turn(blocks)):
        late_tx[q] = block
    early_rx[me] = early_tx[me]
    late_rx[me] = late_tx[me]
    for q in range(n_paths):
        loan_rx[me * n_paths + q] = loan_tx[q]

    for k in range(9, 14):
        loads[k].wait()
    key = (jnp.broadcast_to(owner[...], (deals, deals)) * deals
           + lax.broadcasted_iota(jnp.int32, (deals, deals), 1)).astype(f32)
    key_col = jnp.concatenate([key, jnp.zeros((128 - deals, deals), f32)], axis=0).T[:, :deals]
    below = jnp.where(key_col < key, 1.0, 0.0).astype(f32)
    spot = jnp.sum(below, axis=0, keepdims=True)
    perm = jnp.where(spot == lax.broadcasted_iota(jnp.int32, (deals, deals), 0).astype(f32), 1.0, 0.0).astype(f32)
    listing = jnp.sum(perm * lax.broadcasted_iota(jnp.int32, (deals, deals), 1).astype(f32), axis=1, keepdims=True)

    def spread(x):
        x = jnp.dot(perm, x, preferred_element_type=f32, precision=lax.Precision.HIGHEST)
        x = jnp.concatenate([x, jnp.zeros((deals, 128 - tranches), f32)], axis=1)
        return jnp.concatenate([x] * copies, axis=0).T[:tranches, :]

    table[...] = spread(order[...].astype(f32))
    share_t = spread(share[...])
    rate_t = spread(trate[...])
    names = lax.broadcasted_iota(jnp.int32, (tranches, lanes_out), 0).astype(f32)

    def walk(j, carry):
        run, upto = carry
        hit = names == table[pl.ds(j, 1), :]
        run = run + jnp.sum(jnp.where(hit, share_t, 0.0), axis=0, keepdims=True)
        return run, jnp.where(hit, run, upto)

    whole, upto = lax.fori_loop(
        0, tranches, walk, (jnp.zeros((1, lanes_out), f32), jnp.zeros((tranches, lanes_out), f32)), unroll=4)
    weight = share_t / whole
    upto = upto / whole
    per_weight = 1.0 / weight
    falls[0], falls[1], falls[2], falls[3] = upto, per_weight, rate_t * weight, rate_t

    stack = jnp.concatenate([rates[t] for t in range(steps)] + [jnp.zeros((128 - 2 * steps, paths), f32)], axis=0)
    cols[...] = stack.T
    mine = cols[pl.ds(pl.multiple_of(me * here, here), here), :]
    disc = []
    total = jnp.zeros((here, 1), f32)
    for t in range(steps):
        mort[t] = jnp.broadcast_to((0.5 * incentive) * mine[:, 2 * t + 1:2 * t + 2], (here, 128))
        total = total + (mine[:, 2 * t:2 * t + 1] + oas_spread)
        disc.append(jnp.exp(-total / 12.0))

    for k, copy in enumerate(loan_copies):
        copy.wait_recv()
        for again in pass_copies[k * (n_paths - 1):(k + 1) * (n_paths - 1)]:
            again.start()
    for copy in early_copies:
        copy.wait_send()
    for copy in late_copies:
        copy.start()
    for copy in pass_copies:
        copy.wait_recv()

    ages = lax.broadcasted_iota(jnp.int32, (8, 128), 0).astype(f32)
    listed = jnp.broadcast_to(listing, (deals, 128))

    def prepare(i, carry):
        for k in range(halves):
            lv = loan_rx[i, k]
            r = lv[2:3, :]
            grown = 1.0 + r
            log = jnp.log(grown) * (r / (grown - 1.0))
            x = (lv[4:5, :] - ages) * log
            terms[i, k] = 1.0 - (2.0 * r) / (jnp.exp(x) - 1.0)
            hit = listed == lv[6:7, :]
            high = r.astype(bf16).astype(f32)
            member = jnp.concatenate(
                [jnp.where(hit, 1.0, 0.0), jnp.where(hit, high, 0.0), jnp.where(hit, r - high, 0.0),
                 jnp.zeros((lanes_out - 3 * deals, 128), f32)], axis=0).astype(bf16)
            members[i * halves + k] = member
            for t in range(late):
                late_stay[i, k, t * here:(t + 1) * here, :] = 1.0 - jnp.tanh(lv[0:1, :] - mort[early + t])
        return carry

    lax.fori_loop(0, n_all, prepare, 0, unroll=PREPARE)
    step_scale = -0.5 * price_sens / (fixed_point * 65536.0)

    def pairs(x):
        x = jnp.floor(x * fixed_point + 0.5).astype(jnp.int32)
        return [(x[t * here:(t + 1) * here] << 16) | (x[(t + 1) * here:(t + 2) * here] & 65535)
                for t in range(0, x.shape[0] // here, 2)]

    def months(start, count, tab, cash, acc, found_a, found_b, span):
        height = count * here
        cash[0] = jnp.zeros(cash.shape[1:], bf16)
        acc[...] = jnp.zeros_like(acc)

        sets = n_all // span
        each = span * halves

        def deal_sums(i):
            flat = jnp.concatenate([cash[i, g] for g in range(each)], axis=1)
            base = jnp.maximum(i - 1, 0) * each
            those = jnp.concatenate([members[base + g] for g in range(each)], axis=1)
            return lax.dot_general(flat, those, (((1,), (1,)), ((), ())), preferred_element_type=f32)

        def row(ref, s, k, j):
            return jnp.broadcast_to(ref[s, k, j:j + 1, :], (8, 128))

        def look_up(i, found):
            for g in range(each):
                s, k = i * span + g // halves, g % halves
                lane = row(loan_rx, s, k, 5).astype(jnp.int32)
                home = row(loan_rx, s, k, 7)
                away = [home == float(c) for c in range(1, n_loans)]
                for low in range(0, height // 2, 8):
                    v = None
                    for c in range(n_loans):
                        x = jnp.take_along_axis(tab[c, low:low + 8, :], lane, axis=1, mode="promise_in_bounds")
                        v = x if v is None else jnp.where(away[c - 1], x, v)
                    found[g, low:low + 8, :] = v

        def advance(i, found):
            acc[...] += deal_sums(i)
            for g in range(each):
                s, k = i * span + g // halves, g % halves
                for p in range(0, here, 16):
                    duo = [[], []]
                    for b in range(2):
                        at = p + 8 * b
                        held = row(loan_rx, s, k, 3) if start == 0 else balances[s, k, at:at + 8, :]
                        for two in range(0, count, 2):
                            low = (two // 2) * here + at
                            v = found[g, low:low + 8, :]
                            for t, x in ((two, v & -65536), (two + 1, v << 16)):
                                if start == 0:
                                    stay = 1.0 - jnp.tanh(row(loan_rx, s, k, 0) - mort[t, at:at + 8, :])
                                else:
                                    stay = late_stay[s, k, t * here + at:t * here + at + 8, :]
                                alive = row(terms, s, k, start + t) - jnp.tanh(
                                    row(loan_rx, s, k, 1) + x.astype(f32) * step_scale)
                                held = held * (stay * alive)
                                duo[b].append(held)
                        if start + count < steps:
                            balances[s, k, at:at + 8, :] = held
                    for t in range(count):
                        x = jnp.concatenate([duo[0][t], duo[1][t]], axis=0)
                        high = x.astype(bf16)
                        cash[i + 1, g, t * here + p:t * here + p + 16, :] = high
                        cash[i + 1, g, height + t * here + p:height + t * here + p + 16, :] = (
                            x - high.astype(f32)).astype(bf16)

                if start == 0:
                    x = row(loan_rx, s, k, 3)
                    high = x.astype(bf16).astype(f32)
                    cash[i + 1, g, 2 * height:, :] = jnp.concatenate([high, x - high], axis=0).astype(bf16)

        def two_sets(m, carry):
            look_up(2 * m + 1, found_b)
            advance(2 * m, found_a)
            look_up(2 * m + 2, found_a)
            advance(2 * m + 1, found_b)
            return carry

        look_up(0, found_a)
        lax.fori_loop(0, sets // 2 - 1, two_sets, 0)
        look_up(sets - 1, found_b)
        advance(sets - 2, found_a)
        advance(sets - 1, found_b)
        sums = acc[...] + deal_sums(sets)
        first = sums[2 * height:2 * height + 8] + sums[2 * height + 8:] if start == 0 else None
        sums = sums[:height] + sums[height:2 * height]
        return first, [sums[t * here:(t + 1) * here] * (0.25 ** (start + t + 1)) for t in range(count)]

    sub = here // copies
    group_of = lax.broadcasted_iota(jnp.int32, (sub, lanes_out), 1) // deals

    def packed(x):
        x = jnp.broadcast_to(x, (here, lanes_out))
        y = x[0:sub]
        for c in range(1, copies):
            y = jnp.where(group_of == c, x[c * sub:(c + 1) * sub], y)
        return y

    def shifted(x, column):
        pieces = [x[c * sub:(c + 1) * sub] for c in range(copies)]
        turned = [pltpu.roll(y, ((c - column) % copies) * deals, 1) if (c - column) % copies else y
                  for c, y in enumerate(pieces)]
        y = turned[0]
        for c in range(1, copies):
            y = jnp.where(group_of == c, turned[c], y)
        return y

    fall = [packed(disc[t]) for t in range(steps)]

    def flows(state, sums):
        held, inter, paid_upto = state
        gone, gains = [], []
        for x in sums:
            after = shifted(x, 0)
            paid_upto = paid_upto + jnp.maximum(held - after, 0.0)
            gone.append(paid_upto * per_start)
            gains.append(inter * per_start)
            held, inter = after, shifted(x, 1) + shifted(x, 2)
        return (held, inter, paid_upto), gone, gains

    def line(j, k):
        return jnp.broadcast_to(falls[j, k:k + 1, :], (sub, lanes_out))

    def left_over(k, gone):
        return jnp.clip((line(0, k) - gone) * line(1, k), 0.0, 1.0)

    def settle(first, gone, d, extra):
        dues = [jnp.zeros((sub, lanes_out), f32) for _ in range(4)]
        for k in range(tranches):
            frac = 1.0 if first else fracs[k]
            later = left_over(k, gone)
            w = (frac - later) * d + (line(3, k) * frac) * extra
            worth[k] = w if first else worth[k] + w
            dues[k % 4] = dues[k % 4] + line(2, k) * later
            fracs[k] = later
        return (dues[0] + dues[1]) + (dues[2] + dues[3])

    for copy in early_copies:
        copy.wait_recv()
    tail = jnp.zeros((128 - rows, paths), f32)
    for c in range(n_loans):
        for k, x in enumerate(pairs(jnp.concatenate([early_rx[c], tail], axis=0).T)):
            early_tab[c, k * here:(k + 1) * here, :] = x
    bases, sums = months(0, early, early_tab, early_cash, early_sums, early_a, early_b, EARLY_SPAN)
    bases = jnp.concatenate([bases[:sub]] * copies, axis=0)
    per_start = 1.0 / shifted(bases, 0)
    for copy in late_copies:
        copy.wait_recv()
    lower = late * here
    for c in range(n_loans):
        x = jnp.concatenate([late_rx[c], jnp.zeros((128 - split, paths), f32)], axis=0).T
        upper = pltpu.roll(x[lower:], split, 1)
        late_tab[c] = pairs(jnp.where(lax.broadcasted_iota(jnp.int32, (lower, 128), 1) < split, x[:lower], upper))[0]
    state = (shifted(bases, 0), shifted(bases, 1) + shifted(bases, 2), jnp.zeros((sub, lanes_out), f32))
    state, gone, gains = flows(state, sums)
    dues = jnp.sum(falls[2], axis=0, keepdims=True)
    for t in range(early):
        dues = settle(t == 0, gone[t], fall[t], gains[t] * fall[t] / dues)
    extra = (state[1] * per_start) * fall[early] / dues
    for k in range(tranches):
        worth[k] = worth[k] + fracs[k] * (fall[early] + line(3, k) * extra)

    _, late_totals = months(early, late, late_tab, late_cash, late_sums, late_a, late_b, LATE_SPAN)
    state, gone, gains = flows(state, late_totals)
    dues = [jnp.zeros((sub, lanes_out), f32) for _ in range(4)]
    for k in range(tranches):
        later = left_over(k, gone[0])
        dues[k % 4] = dues[k % 4] + line(2, k) * later
        fracs[k] = later
    extra = gains[1] * fall[steps - 1] / ((dues[0] + dues[1]) + (dues[2] + dues[3]))
    total = []
    for k in range(tranches):
        frac = fracs[k]
        later = left_over(k, gone[1])
        w = (worth[k] - frac * fall[early] + (frac - later) * fall[steps - 1]
             + (line(3, k) * frac) * extra + later * fall[steps - 1])
        total.append(jnp.sum(w, axis=0, keepdims=True))

    wt = jnp.concatenate(total + [jnp.zeros((128 - tranches, lanes_out), f32)], axis=0).T
    acc = wt[0:deals]
    low = lax.broadcasted_iota(jnp.int32, (deals // 2, 128), 1) < 64
    for c in range(1, copies):
        acc = acc + wt[c * deals:(c + 1) * deals]
    acc = jnp.where(low, acc[:deals // 2], pltpu.roll(acc[deals // 2:], 64, 1))
    part[...] = acc
    part_copies = []
    for off in range(1, n_all):
        part_copies.append(pltpu.make_async_remote_copy(
            src_ref=part, dst_ref=part_rx.at[rank], send_sem=part_ss.at[off], recv_sem=part_rs.at[off],
            device_id=other(off), device_id_type=MESH))
    for copy in part_copies:
        copy.start()
    part_rx[rank] = acc
    for copy in part_copies:
        copy.wait_recv()
    acc = part_rx[0]
    for k in range(1, n_all):
        acc = acc + part_rx[k]
    acc = 100.0 * (acc / (paths * n_paths) - 1.0)
    out[:deals // 2, :] = acc[:, :tranches]
    out[deals // 2:, :] = pltpu.roll(acc, 64, 1)[:, :tranches]
    for copy in loan_copies + pass_copies + late_copies + part_copies:
        copy.wait_send()


def fused(loan_features, hazard_coef, coupon, balance, loan_term, loan_age, loan_region, loan_deal,
          region_hpi, rate_paths, deal_owner, tranche_order, tranche_share, tranche_rate):
    n_loans, n_paths = lax.axis_size("loans"), lax.axis_size("paths")
    n = coupon.shape[0]
    rows, steps, paths = region_hpi.shape
    deals, tranches = tranche_share.shape
    here = paths // n_loans
    lanes_out = 128
    split = -(-rows // 16) * 8
    early, late = n_loans, steps - n_loans
    halves = n // n_paths // 128
    n_all = n_loans * n_paths
    f32, bf16 = jnp.float32, jnp.bfloat16
    dma = pltpu.SemaphoreType.DMA
    operands = (loan_features, hazard_coef.T, rows_of(coupon), rows_of(balance), rows_of(loan_term), rows_of(loan_age),
                rows_of(loan_region), rows_of(loan_deal), region_hpi.transpose(1, 0, 2),
                rate_paths.transpose(1, 0, 2), deal_owner.reshape(1, deals), tranche_order, tranche_share, tranche_rate)
    return pl.pallas_call(
        functools.partial(pool_kernel, (n_loans, n_paths), lanes_out),
        out_shape=pltpu.VMEM((deals, tranches), f32),
        in_specs=[pl.BlockSpec(memory_space=pl.ANY)] * len(operands),
        out_specs=pl.BlockSpec(memory_space=pltpu.VMEM),
        scratch_shapes=[pltpu.VMEM(x.shape, x.dtype) for x in operands] + [
            pltpu.VMEM((n_paths, halves, 8, 128), f32),
            pltpu.VMEM((n_all, halves, 8, 128), f32),
            pltpu.VMEM((n_loans, rows, paths), f32),
            pltpu.VMEM((n_loans, rows, paths), f32),
            pltpu.VMEM((n_loans, split, paths), f32),
            pltpu.VMEM((n_loans, split, paths), f32),
            pltpu.VMEM((n_loans, early // 2 * here, 128), jnp.int32),
            pltpu.VMEM((n_loans, late // 2 * here, 128), jnp.int32),
            pltpu.VMEM((steps, here, 128), f32),
            pltpu.VMEM((n_all, halves, 8, 128), f32),
            pltpu.VMEM((n_all, halves, late * here, 128), f32),
            pltpu.VMEM((n_all * halves, lanes_out, 128), bf16),
            pltpu.VMEM((n_all, halves, here, 128), f32),
            pltpu.VMEM((n_all // EARLY_SPAN + 1, EARLY_SPAN * halves, 2 * early * here + 16, 128), bf16),
            pltpu.VMEM((n_all // LATE_SPAN + 1, LATE_SPAN * halves, 2 * late * here, 128), bf16),
            pltpu.VMEM((2 * early * here + 16, lanes_out), f32),
            pltpu.VMEM((2 * late * here, lanes_out), f32),
            pltpu.VMEM((EARLY_SPAN * halves, early // 2 * here, 128), jnp.int32),
            pltpu.VMEM((EARLY_SPAN * halves, early // 2 * here, 128), jnp.int32),
            pltpu.VMEM((LATE_SPAN * halves, late // 2 * here, 128), jnp.int32),
            pltpu.VMEM((LATE_SPAN * halves, late // 2 * here, 128), jnp.int32),
            pltpu.VMEM((tranches, here * deals // lanes_out, lanes_out), f32),
            pltpu.VMEM((4, tranches, lanes_out), f32),
            pltpu.VMEM((tranches, here * deals // lanes_out, lanes_out), f32),
            pltpu.VMEM((tranches, lanes_out), f32),
            pltpu.VMEM((paths, 128), f32),
            pltpu.VMEM((deals // 2, 128), f32),
            pltpu.VMEM((n_all, deals // 2, 128), f32),
            dma((len(operands),)),
            dma((n_loans,)), dma((n_loans,)), dma((n_loans, n_paths)), dma((n_loans, n_paths)),
            dma((n_loans,)), dma((n_loans,)), dma((n_loans,)), dma((n_loans,)),
            dma((n_all,)), dma((n_all,)),
        ],
        compiler_params=pltpu.CompilerParams(collective_id=0, has_side_effects=True),
    )(*operands)


def fits(args):
    n = args[2].shape[0]
    paths = args[8].shape[2]
    deals, tranches = args[12].shape
    n_loans = lax.axis_size("loans")
    rows, steps = args[8].shape[:2]
    return (
        paths == 128 and n_loans == 4 and 2 * (steps - n_loans) == n_loans and rows % 8 == 0 and 64 < rows <= 128
        and deals in (16, 32) and tranches == 64
        and (paths // n_loans) % (8 * (128 // deals)) == 0
        and n % (128 * lax.axis_size("paths")) == 0 and n <= 2048
    )


def device_program(*args):
    return fused(*args) if fits(args) else on_device(*args)


def solution(mesh):
    in_specs = (
        P(("groups", "loans"), None),
        P(),
        P(("groups", "loans")),
        P(("groups", "loans")),
        P(("groups", "loans")),
        P(("groups", "loans")),
        P(("groups", "loans")),
        P(("groups", "loans")),
        P(("groups", "loans"), None, "paths"),
        P(None, None, ("groups", "paths")),
        P("groups", None),
        P("groups", None),
        P("groups", None),
        P("groups", None),
    )
    out_specs = P("groups", None)
    return jax.shard_map(
        device_program, mesh=mesh, in_specs=in_specs, out_specs=out_specs, check_vma=False
    )
```
